256 devices in a mesh: seq: 32 (over z, x), expert: 8 (over y, core).
Axes of the slice: x: 4, y: 4, z: 8, core: 2. Of those that a mesh axis runs over, the one named last changes fastest.
Arguments:
- tokens: bfloat16 [4096, 4096], P('seq'), may hold values from -6 to 6
- norm_gain: float32 [4096], replicated, may hold values from 0.1 to 1.9
- router_weight: bfloat16 [4096, 8], replicated, may hold values from -0.09375 to 0.09375
- expert_ids: int32 [4096, 2], P('seq'), may hold values from 0 to 7, all different within a row; in each aligned block of 128 rows (0 to 127, 128 to 255, ...) at most 40 rows name the same one
- gate_weight: bfloat16 [8, 4096, 8192], P('expert', None, 'seq'), may hold values from -0.09375 to 0.09375
- up_weight: bfloat16 [8, 4096, 8192], P('expert', None, 'seq'), may hold values from -0.09375 to 0.09375
- down_weight: bfloat16 [8, 8192, 4096], P('expert', 'seq'), may hold values from -0.0625 to 0.0625
- query_weight: bfloat16 [4096, 2048], P(None, 'expert'), may hold values from -0.09375 to 0.09375
- key_weight: bfloat16 [4096, 2048], P(None, 'expert'), may hold values from -0.09375 to 0.09375
- log_decay: float32 [32, 4096], P('expert', 'seq'), may hold values from -1.5 to 0
- carried_state: float32 [32, 64, 128], P('expert'), may hold values from -48 to 48
- out_gain: float32 [4096], P('expert'), may hold values from 0.1 to 1.9
Outputs:
- teacher_out: bfloat16 [4096, 4096], P('seq', 'expert')
- student_out: bfloat16 [4096, 4096], P('seq', 'expert')
- token_loss: float32 [4096], P('seq')
The draws below stay inside these ranges and needn't reach their ends.
Inputs may be any that keep to these rules, and one draw needn't show every extreme that they name: `expert_ids`: each token names 2 different experts. Among the 128 tokens of one block no expert is named by more than 40 tokens, and in every draw some expert is named by exactly 40 tokens of some block.
All inputs are finite; a program needn't handle non-finite values.
Results may differ from the reference program's by a relative error of at most 0.01.
Values may be sent and summed in bfloat16 or wider, within the bound.
No kernel may reach another device: no remote copies, remote signals or barrier semaphores. Data moves between devices by JAX's collectives and lax.ppermute only.
A program may use at most 128 MiB of HBM per device.

```python
import math
import jax
import jax.numpy as jnp
import numpy as np
from jax import lax

D = 4096
EXPERTS = 8
TOP = 2
FF = 8192
SPAN = 128
TOKEN_LENGTH = 4096
CAP = 28
LOAD = 40
HEAD = 128
KEY = 64
STUDENT_HEADS = 32
N_SEQ = 32


def draw_log_decay(key, part):
    key_sequence = jax.random.split(jax.random.fold_in(key, 17), 7)
    fast_share = 0.5
    blocks = TOKEN_LENGTH // SPAN
    fast_pick = jax.random.uniform(key_sequence[0], (STUDENT_HEADS, 1), jnp.float32) < fast_share
    fast_rate = jnp.exp(jax.random.uniform(key_sequence[1], (STUDENT_HEADS, 1), jnp.float32, jnp.log(1.0 / 50.0), jnp.log(1.0 / 30.0)))
    slow_rate = jnp.exp(jax.random.uniform(key_sequence[2], (STUDENT_HEADS, 1), jnp.float32, jnp.log(0.3), jnp.log(0.6))) / TOKEN_LENGTH
    base_rate = jnp.where(fast_pick, fast_rate, slow_rate)
    block_factor = jnp.exp(jax.random.uniform(key_sequence[3], (STUDENT_HEADS, blocks, 1), jnp.float32, jnp.log(0.7), jnp.log(1.5)))
    roughness = jax.random.uniform(key_sequence[4], (STUDENT_HEADS, blocks, SPAN), jnp.float32, 0.5, 1.5)
    decay_rates = (base_rate[:, :, None] * block_factor * roughness).reshape(STUDENT_HEADS, TOKEN_LENGTH)
    spike_position = jax.random.randint(key_sequence[5], (STUDENT_HEADS, 3, 1), 0, TOKEN_LENGTH)
    spike_loss = jax.random.uniform(key_sequence[6], (STUDENT_HEADS, 3, 1), jnp.float32, jnp.log(0.65), jnp.log(0.8))
    token_positions = jnp.arange(TOKEN_LENGTH)[None, None, :]
    spike_tokens = jnp.sum(jnp.where(token_positions == spike_position, spike_loss, 0.0), axis=1)
    return (spike_tokens - decay_rates).astype(jnp.float32)


def block_scale(key, extent, pieces, smallest, largest):
    level = 1.0
    for position, blocks in pieces:
        steps = jax.random.uniform(jax.random.fold_in(jax.random.fold_in(key, 6), position), (blocks,), jnp.float32, smallest / len(pieces), largest / len(pieces))
        level = level * jnp.repeat(jnp.exp(steps), extent[position] // blocks).reshape((-1,) + (1,) * (len(extent) - 1 - position))
    return level


def routed_block(rng, own, number, rows, count, top, bound, slope):
    order = jax.random.permutation(rng, count)
    crowded, common = load_shares(count, rows * top, bound, slope, True), load_shares(count, rows * top, bound, slope, False)
    places = jnp.arange(count)

    def named(lengths, offset_by):
        used = int((lengths > 0).sum())
        fixed = max(1, used // 4)
        passed = fixed + (places - fixed + offset_by * (used - fixed)) % max(1, count - fixed)
        return jnp.zeros((count,), jnp.int32).at[order[jnp.where(places < fixed, places, passed)]].set(jnp.asarray(lengths, jnp.int32))

    lengths = jnp.where(number % 4 == 0, named(crowded, number // 4), named(common, number - number // 4 - 1))
    mixed = jax.random.permutation(jax.random.fold_in(own, 3), count)
    source_of, sink = mixed[0:count // 2 * 2:2], mixed[1:count // 2 * 2:2]
    margin = jnp.minimum(lengths[source_of] - 1, bound - lengths[sink]) // 2
    margin = jnp.where((source_of == order[0]) | (sink == order[0]) | (lengths[sink] == 0), 0, jnp.maximum(margin, 0))
    passed = jax.random.randint(jax.random.fold_in(own, 4), (count // 2,), 0, 1 << 20) % (margin + 1)
    lengths = lengths.at[source_of].add(-passed).at[sink].add(passed)
    items = jnp.searchsorted(jnp.cumsum(lengths), jnp.arange(rows * top), side="right").astype(jnp.int32)
    listing = items.reshape(top, rows).T
    listing = listing[jax.random.permutation(jax.random.fold_in(own, 1), rows)]
    offset_by = jax.random.randint(jax.random.fold_in(own, 2), (rows, 1), 0, top)
    return jnp.take_along_axis(listing, (jnp.arange(top)[None, :] + offset_by) % top, axis=1)


def load_shares(count, total, limit, lean, full):
    loads = [(1 << 20) // math.isqrt(rank ** lean) + 1 for rank in range(1, count + 1)]
    largest = limit if full else min(limit, max(-(-total // count), total * loads[0] // sum(loads)))
    least = 1 if total - largest >= count - 1 else 0
    counts, spare = [largest] + [least] * (count - 1), total - largest - least * (count - 1)
    while spare > 0:
        candidates = [i for i in range(1, count) if counts[i] < largest] or [i for i in range(1, count) if counts[i] < limit]
        pool, budget = sum([loads[i] for i in candidates]), spare
        for i in candidates:
            extra = min(limit - counts[i], max(1, budget * loads[i] // pool), spare)
            counts[i] = counts[i] + extra
            spare = spare - extra
    return np.array(counts)


def noise(rng, shape, scale, limit, pieces=(), kind=jnp.bfloat16):
    result = scale * jax.random.normal(rng, shape, jnp.float32)
    if pieces:
        result = result * block_scale(rng, shape, pieces, -0.22, 0.18)
    return jnp.clip(result, -limit, limit).astype(kind)


def setup_inputs(seed: int = 0) -> dict:
    splits = jax.random.split(jax.random.key(seed), 13)
    tokens = noise(splits[0], (TOKEN_LENGTH, D), 1.0, 6.0, ((0, 32),))
    norm_gain = jnp.clip(1.0 + 0.18 * jax.random.normal(splits[1], (D,), jnp.float32), 0.1, 1.9)
    router_weight = noise(splits[2], (D, EXPERTS), D ** -0.5, 0.09375)
    expert_ids_keys = jax.random.split(jax.random.fold_in(splits[3], 1), TOKEN_LENGTH // SPAN)
    expert_ids_turns = jax.random.permutation(jax.random.fold_in(splits[3], 3), TOKEN_LENGTH // SPAN)
    expert_ids = jax.vmap(lambda own, number: routed_block(jax.random.fold_in(splits[3], 2), own, number, SPAN, EXPERTS, TOP, LOAD, 1))(expert_ids_keys, expert_ids_turns).reshape((TOKEN_LENGTH, TOP))
    gate_weight = noise(splits[4], (EXPERTS, D, FF), D ** -0.5, 0.09375, ((0, 8), (2, 32)))
    up_weight = noise(splits[5], (EXPERTS, D, FF), D ** -0.5, 0.09375, ((0, 8), (2, 32)))
    down_weight = noise(splits[6], (EXPERTS, FF, D), FF ** -0.5, 0.0625, ((0, 8), (1, 32)))
    query_weight = noise(splits[7], (D, STUDENT_HEADS * KEY), D ** -0.5, 0.09375, ((1, 8),))
    key_weight = noise(splits[8], (D, STUDENT_HEADS * KEY), D ** -0.5, 0.09375, ((1, 8),))
    log_decay = draw_log_decay(jax.random.fold_in(splits[12], 71), 0)
    carried_state = noise(splits[10], (STUDENT_HEADS, KEY, HEAD), 8.0, 48.0, ((0, 8),), jnp.float32)
    out_gain = jnp.clip(1.0 + 0.18 * jax.random.normal(splits[11], (D,), jnp.float32), 0.1, 1.9)
    return {"tokens": tokens, "norm_gain": norm_gain, "router_weight": router_weight, "expert_ids": expert_ids, "gate_weight": gate_weight, "up_weight": up_weight, "down_weight": down_weight, "query_weight": query_weight, "key_weight": key_weight, "log_decay": log_decay, "carried_state": carried_state, "out_gain": out_gain}


norm_epsilon = 1e-05
head_epsilon = 1e-06
peak_error = lax.Precision.HIGHEST

def reference(tokens, norm_gain, router_weight, expert_ids, gate_weight, up_weight, down_weight, query_weight, key_weight, log_decay, carried_state, out_gain):
    tok_float = tokens.astype(jnp.float32)
    normed = (tok_float * lax.rsqrt(lax.optimization_barrier(jnp.mean(tok_float * tok_float, axis=1, keepdims=True)) + norm_epsilon) * norm_gain).astype(jnp.bfloat16)
    logits = jnp.dot(normed, router_weight, preferred_element_type=jnp.float32)
    expert_iota = jnp.arange(EXPERTS, dtype=jnp.int32)
    picks = expert_ids[:, :, None] == expert_iota[None, None, :]
    chosen = lax.optimization_barrier(jnp.sum(jnp.where(picks, logits[:, None, :], jnp.float32(0.0)), axis=2))
    first_share = 1.0 / (1.0 + jnp.exp(chosen[:, 1] - chosen[:, 0]))
    shares = jnp.stack([first_share, 1.0 - first_share], axis=1)
    mix_weight = lax.optimization_barrier(jnp.sum(jnp.where(picks, shares[:, :, None], jnp.float32(0.0)), axis=1))
    hits = jnp.any(picks, axis=1).astype(jnp.int32)
    blocks = TOKEN_LENGTH // SPAN
    block_hits = hits.reshape(blocks, SPAN, EXPERTS)
    block_slots = jnp.cumsum(block_hits, axis=1) - block_hits
    block_weight = mix_weight.reshape(blocks, SPAN, EXPERTS)
    slot_iota = jnp.arange(CAP, dtype=jnp.int32)
    normed_blocks = normed.reshape(blocks, SPAN, D).astype(jnp.float32)
    ff_part = FF // N_SEQ

    def one_expert(mixed, inputs):
        expert_index, gate_mat, up_mat, down_mat = inputs
        chosen_col = expert_iota[None, None, :] == expert_index
        own_hits = lax.optimization_barrier(jnp.sum(jnp.where(chosen_col, block_hits, 0), axis=2))
        own_slots = lax.optimization_barrier(jnp.sum(jnp.where(chosen_col, block_slots, 0), axis=2))
        own_weight = lax.optimization_barrier(jnp.sum(jnp.where(chosen_col, block_weight, jnp.float32(0.0)), axis=2))
        select = ((own_hits[:, None, :] == 1) & (own_slots[:, None, :] == slot_iota[None, :, None])).astype(jnp.float32)
        rows = jnp.einsum('cpt,ctd->cpd', select, normed_blocks, precision=peak_error).astype(jnp.bfloat16).reshape(blocks * CAP, D)
        gate_proj = jnp.dot(rows, gate_mat, preferred_element_type=jnp.float32)
        up_proj = jnp.dot(rows, up_mat, preferred_element_type=jnp.float32)
        hidden = (jax.nn.silu(gate_proj) * up_proj).astype(jnp.bfloat16)

        def add_part(total, part_index):
            hidden_part = lax.dynamic_slice_in_dim(hidden, part_index * ff_part, ff_part, 1)
            down_part = lax.dynamic_slice_in_dim(down_mat, part_index * ff_part, ff_part, 0)
            partial_value = jnp.dot(hidden_part, down_part, preferred_element_type=jnp.float32).astype(jnp.bfloat16)
            partial_value = lax.optimization_barrier(partial_value)
            return (total + partial_value.astype(jnp.float32), None)
        total, _ = lax.scan(add_part, jnp.zeros((blocks * CAP, D), jnp.float32), jnp.arange(N_SEQ, dtype=jnp.int32))
        rounded = lax.optimization_barrier(total.astype(jnp.bfloat16))
        expert_rows = rounded.astype(jnp.float32).reshape(blocks, CAP, D)
        weigh = select * own_weight[:, None, :]
        spread = jnp.einsum('cpt,cpd->ctd', weigh, expert_rows, precision=peak_error).reshape(TOKEN_LENGTH, D)
        return (mixed + spread, None)
    mixed, _ = lax.scan(one_expert, jnp.zeros((TOKEN_LENGTH, D), jnp.float32), (expert_iota, gate_weight, up_weight, down_weight))
    teacher_hidden = tok_float + mixed

    def to_blocks(matrix, features):
        return matrix.reshape(TOKEN_LENGTH, STUDENT_HEADS, features).transpose(1, 0, 2).reshape(STUDENT_HEADS, blocks, SPAN, features).transpose(1, 0, 2, 3)
    query_rows = to_blocks(jnp.dot(tokens, query_weight, preferred_element_type=jnp.float32), KEY)
    keys_proj = to_blocks(jnp.dot(tokens, key_weight, preferred_element_type=jnp.float32), KEY)
    value_rows = to_blocks(tok_float, HEAD)
    decays = log_decay.reshape(STUDENT_HEADS, blocks, SPAN).transpose(1, 0, 2)
    lower = jnp.arange(SPAN)[:, None] >= jnp.arange(SPAN)[None, :]

    def one_block(recurrent_state, inputs):
        query_block, block_k, value_block, block_g = inputs
        running_state = jnp.cumsum(block_g, axis=1)
        last_state = running_state[:, -1]
        gaps = running_state[:, :, None] - running_state[:, None, :]
        weights = jnp.where(lower[None], jnp.exp(jnp.minimum(gaps, 0.0)), 0.0)
        scores = jnp.einsum('htk,hsk->hts', query_block, block_k, precision=peak_error) * weights
        output_rows = jnp.einsum('hts,hsv->htv', scores, value_block, precision=peak_error)
        output_rows = output_rows + jnp.exp(running_state)[:, :, None] * jnp.einsum('ezy,eyl->ezl', query_block, recurrent_state, precision=peak_error)
        scaled_keys = block_k * jnp.exp(last_state[:, None] - running_state)[:, :, None]
        recurrent_state = jnp.exp(last_state)[:, None, None] * recurrent_state + jnp.einsum('wpl,wpg->wlg', scaled_keys, value_block, precision=peak_error)
        return (recurrent_state, output_rows)
    _, output_rows = lax.scan(one_block, carried_state.astype(jnp.float32), (query_rows, keys_proj, value_rows, decays))
    normed_out = output_rows * lax.rsqrt(lax.optimization_barrier(jnp.mean(output_rows * output_rows, axis=3, keepdims=True)) + head_epsilon)
    branch = normed_out.transpose(0, 2, 1, 3).reshape(TOKEN_LENGTH, D) * out_gain
    student_hidden = tok_float + branch
    gap = student_hidden - teacher_hidden
    token_loss = lax.optimization_barrier(jnp.mean(gap * gap, axis=1))
    return (teacher_hidden.astype(jnp.bfloat16), student_hidden.astype(jnp.bfloat16), token_loss)
```

```python
import functools

import jax
import jax.numpy as jnp
from jax import lax
from jax.experimental import pallas as pl
from jax.experimental.pallas import tpu as pltpu
from jax.sharding import Mesh
from jax.sharding import PartitionSpec as P

SEQ = ("z", "x")
ROWS_A = 16

norm_epsilon = 1e-05
head_epsilon = 1e-06
peak_error = lax.Precision.HIGHEST
F32 = jnp.float32
BF16 = jnp.bfloat16


def shift(value, axis, step, wrap=True):
    n = lax.axis_size(axis)
    pairs = [(i, (i + step) % n) for i in range(n) if wrap or 0 <= i + step < n]
    return lax.ppermute(value, axis, pairs)


def add(*terms):
    return sum(t.astype(F32) for t in terms).astype(BF16)


def mlp_kernel(n, steps, *refs):
    x_refs, (gate_ref, up_ref, down_ref) = refs[:n], refs[n : n + 3]
    out_refs = refs[n + 3 : 2 * n + 3]
    rest = refs[2 * n + 3 :]
    gates, ups, hiddens = rest[:n], rest[n : 2 * n], rest[2 * n :]
    i = pl.program_id(0)

    @pl.when(i == 0)
    def _():
        for k in range(n):
            gates[k][...] = jnp.dot(x_refs[k][...], gate_ref[0], preferred_element_type=F32)
            ups[k][...] = jnp.dot(x_refs[k][...], up_ref[0], preferred_element_type=F32)

    @pl.when((i > 0) & (i < steps))
    def _():
        for k in range(n):
            gates[k][...] += jnp.dot(x_refs[k][...], gate_ref[0], preferred_element_type=F32)
            ups[k][...] += jnp.dot(x_refs[k][...], up_ref[0], preferred_element_type=F32)

    @pl.when(i == steps - 1)
    def _():
        for k in range(n):
            v = gates[k][...]
            hiddens[k][...] = (v / (1.0 + jnp.exp(-v)) * ups[k][...]).astype(BF16)

    @pl.when(i >= steps)
    def _():
        for k in range(n):
            out_refs[k][...] = jnp.dot(
                hiddens[k][...], down_ref[0], preferred_element_type=F32
            ).astype(BF16)


def mlp(rows, gate, up, down):
    n = len(rows)
    width, hidden = gate.shape[1], gate.shape[2]
    steps = 4
    tile = width // steps
    first = lambda i: jnp.minimum(i, steps - 1)
    second = lambda i: jnp.maximum(i - steps, 0)
    total = sum(r.shape[0] for r in rows)
    return pl.pallas_call(
        functools.partial(mlp_kernel, n, steps),
        grid=(2 * steps,),
        in_specs=[pl.BlockSpec((r.shape[0], tile), lambda i: (0, first(i))) for r in rows]
        + [
            pl.BlockSpec((1, tile, hidden), lambda i: (0, first(i), 0)),
            pl.BlockSpec((1, tile, hidden), lambda i: (0, first(i), 0)),
            pl.BlockSpec((1, hidden, tile), lambda i: (0, 0, second(i))),
        ],
        out_specs=[pl.BlockSpec((r.shape[0], tile), lambda i: (0, second(i))) for r in rows],
        out_shape=[jax.ShapeDtypeStruct(r.shape, BF16) for r in rows],
        scratch_shapes=[pltpu.VMEM((r.shape[0], hidden), F32) for r in rows] * 2
        + [pltpu.VMEM((r.shape[0], hidden), BF16) for r in rows],
        compiler_params=pltpu.CompilerParams(vmem_limit_bytes=40 << 20),
        cost_estimate=pl.CostEstimate(
            flops=6 * total * width * hidden,
            bytes_accessed=4 * total * width + 6 * width * hidden,
            transcendentals=total * hidden,
        ),
    )(*rows, gate, up, down)


def gather_z_by_hops(own):
    up1, down1 = shift(own, "z", 1), shift(own, "z", -1)
    up2, down2 = shift(up1, "z", 1), shift(down1, "z", -1)
    up3, down3 = shift(up2, "z", 1), shift(down2, "z", -1)
    up4 = shift(up3, "z", 1)
    return jnp.concatenate([own, up1, down1, up2, down2, up3, down3, up4])


def scatter_z_by_hops(parts):
    own, up1, down1, up2, down2, up3, down3, up4 = jnp.split(parts, 8)
    back = shift(up4, "z", -1)
    fore = shift(down3, "z", 1)
    back = shift(add(up3, back), "z", -1)
    fore = shift(add(down2, fore), "z", 1)
    back = shift(add(up2, back), "z", -1)
    fore = shift(add(down1, fore), "z", 1)
    back = shift(add(up1, back), "z", -1)
    return add(own, back, fore)


def split_log(value):
    high = lax.reduce_precision(value, 8, 7)
    middle = lax.reduce_precision(value - high, 8, 7)
    return jnp.stack([high, middle, value - high - middle], axis=1)


def pack(state, log):
    heads, keys, size = state.shape
    logs = jnp.broadcast_to(split_log(log)[:, :, None], (heads, 3, size))
    logs = jnp.pad(logs, ((0, 0), (0, 13), (0, 0)))
    return jnp.concatenate([state, logs], axis=1).astype(BF16)


def unpack(packed):
    both = packed.astype(F32)
    return both[:, :-16], both[:, -16, 0] + both[:, -15, 0] + both[:, -14, 0]


def prefix_over_seq(state, log):
    x = lax.axis_index("x")
    packed = pack(state, log)
    parts = [unpack(packed)] + [unpack(shift(packed, "x", k)) for k in (1, 2, 3)]
    places = [lax.rem(x + 4 - k, 4) for k in range(4)]
    total_state = jnp.zeros_like(state)
    inside_state = jnp.zeros_like(state)
    inside_log = jnp.zeros_like(log)
    total_log = jnp.zeros_like(log)
    for k in range(4):
        after = jnp.zeros_like(log)
        within = jnp.zeros_like(log)
        for m in range(4):
            later = places[m] > places[k]
            after = after + jnp.where(later, parts[m][1], 0.0)
            within = within + jnp.where(later & (places[m] < x), parts[m][1], 0.0)
        total_state = total_state + jnp.exp(after)[:, None, None] * parts[k][0]
        total_log = total_log + parts[k][1]
        early = places[k] < x
        inside_state = inside_state + jnp.where(
            early, jnp.exp(within)[:, None, None] * parts[k][0], 0.0
        )
        inside_log = inside_log + jnp.where(early, parts[k][1], 0.0)
    run_packed = shift(pack(total_state, total_log), "z", 1, wrap=False)
    run_state, run_log = unpack(run_packed)
    for step in (1, 2, 4):
        before_state, before_log = unpack(shift(run_packed, "z", step, wrap=False))
        run_state = jnp.exp(run_log)[:, None, None] * before_state + run_state
        run_log = run_log + before_log
        if step < 4:
            run_packed = pack(run_state, run_log)
    state = jnp.exp(inside_log)[:, None, None] * run_state + inside_state
    return state, run_log + inside_log


def over_copies(value, axis):
    copies = jnp.broadcast_to(value, (lax.axis_size(axis), *value.shape))
    return lax.all_to_all(copies, axis, split_axis=0, concat_axis=0, tiled=True).sum(axis=0)


def on_device(
    tokens,
    norm_gain,
    router_weight,
    expert_ids,
    gate_weight,
    up_weight,
    down_weight,
    query_weight,
    key_weight,
    log_decay,
    carried_state,
    out_gain,
):
    span_rows = tokens.shape[0]
    width = tokens.shape[1]
    expert_count = router_weight.shape[1]
    top_count = expert_ids.shape[1]
    capacity = 7 * top_count * span_rows // (8 * expert_count)
    groups = lax.axis_size("expert")
    mine = lax.axis_index("expert")
    block_cols = width // groups
    tok_float = tokens.astype(F32)
    normed = (
        tok_float
        * lax.rsqrt(jnp.mean(tok_float * tok_float, axis=1, keepdims=True) + norm_epsilon)
        * norm_gain
    ).astype(BF16)
    logits = jnp.dot(normed, router_weight, preferred_element_type=F32)
    expert_iota = jnp.arange(expert_count, dtype=jnp.int32)
    picks = expert_ids[:, :, None] == expert_iota[None, None, :]
    chosen = jnp.sum(jnp.where(picks, logits[:, None, :], F32(0.0)), axis=2)
    first_share = 1.0 / (1.0 + jnp.exp(chosen[:, 1] - chosen[:, 0]))
    shares = jnp.stack([first_share, 1.0 - first_share], axis=1)
    mix_weight = jnp.sum(jnp.where(picks, shares[:, :, None], F32(0.0)), axis=1)
    hits = jnp.any(picks, axis=1).astype(jnp.int32)
    slots = jnp.cumsum(hits, axis=0) - hits
    slot_iota = jnp.arange(capacity, dtype=jnp.int32)
    own_col = expert_iota[None, :] == mine
    own_hits = jnp.sum(jnp.where(own_col, hits, 0), axis=1)
    own_slots = jnp.sum(jnp.where(own_col, slots, 0), axis=1)
    select_own = (own_hits[None, :] == 1) & (own_slots[None, :] == slot_iota[:, None])
    dispatched = jnp.dot(
        select_own.astype(BF16), normed, preferred_element_type=F32
    ).astype(BF16)

    own_a, own_b = dispatched[:ROWS_A], dispatched[ROWS_A:]
    rows_a = jnp.concatenate(
        [own_a, shift(own_a, "x", 1), shift(own_a, "x", -1), shift(own_a, "x", 2)]
    )
    rows_a = lax.all_gather(rows_a, "z", axis=0, tiled=True)
    rows_b = gather_z_by_hops(own_b)
    half = rows_b.shape[0] // 2
    rows_p, rows_m = shift(rows_b, "x", 1), shift(rows_b, "x", -1)
    rows_o1, rows_o2 = shift(rows_p[:half], "x", 1), shift(rows_m[half:], "x", -1)

    weights = (gate_weight, up_weight, down_weight)
    part_b, part_p, part_m = mlp([rows_b, rows_p, rows_m], *weights)
    part_o1, part_o2 = mlp([rows_o1, rows_o2], *weights)
    (part_a,) = mlp([rows_a], *weights)

    relay_p, relay_m = shift(part_o1, "x", -1), shift(part_o2, "x", 1)
    rest_p, rest_m = shift(part_p[half:], "x", -1), shift(part_m[:half], "x", 1)
    lead_p = shift(add(part_p[:half], relay_p), "x", -1)
    lead_m = shift(add(part_m[half:], relay_m), "x", 1)
    sum_b = jnp.concatenate(
        [add(part_b[:half], lead_p, rest_m), add(part_b[half:], rest_p, lead_m)]
    )
    sum_b = scatter_z_by_hops(sum_b)
    sum_a = lax.psum_scatter(part_a, "z", scatter_dimension=0, tiled=True)
    sum_0, sum_p, sum_m, sum_o = jnp.split(sum_a, 4)
    sum_a = add(sum_0, shift(sum_p, "x", -1), shift(sum_m, "x", 1), shift(sum_o, "x", 2))
    expert_half = jnp.concatenate([sum_a, sum_b])

    pieces = expert_half.reshape(1, capacity, groups, block_cols)
    arrived = lax.all_to_all(pieces, "expert", split_axis=2, concat_axis=0, tiled=True).reshape(
        groups, capacity, block_cols
    )
    select_all = (hits.T[:, None, :] == 1) & (slots.T[:, None, :] == slot_iota[None, :, None])
    weigh_all = select_all.astype(F32) * mix_weight.T[:, None, :]
    mixed = jnp.einsum("ept,epd->td", weigh_all, arrived.astype(F32), precision=peak_error)
    tok_cols = lax.dynamic_slice_in_dim(tok_float, mine * block_cols, block_cols, 1)
    teacher_hidden = tok_cols + mixed
    heads_local = log_decay.shape[0]
    key_size = query_weight.shape[1] // heads_local
    head_size = block_cols // heads_local
    query_rows = (
        jnp.dot(tokens, query_weight, preferred_element_type=F32)
        .reshape(span_rows, heads_local, key_size)
        .transpose(1, 0, 2)
    )
    keys_proj = (
        jnp.dot(tokens, key_weight, preferred_element_type=F32)
        .reshape(span_rows, heads_local, key_size)
        .transpose(1, 0, 2)
    )
    value_rows = tok_cols.reshape(span_rows, heads_local, head_size).transpose(1, 0, 2)
    running_state = jnp.cumsum(log_decay, axis=1)
    last_state = running_state[:, -1]
    lower = jnp.arange(span_rows)[:, None] >= jnp.arange(span_rows)[None, :]
    gaps = running_state[:, :, None] - running_state[:, None, :]
    weights = jnp.where(lower[None], jnp.exp(jnp.minimum(gaps, 0.0)), 0.0)
    scores = jnp.einsum("htk,hsk->hts", query_rows, keys_proj, precision=peak_error) * weights
    output_rows = jnp.einsum("hts,hsv->htv", scores, value_rows, precision=peak_error)
    scaled_keys = keys_proj * jnp.exp(last_state[:, None] - running_state)[:, :, None]
    block_state = jnp.einsum("wpl,wpg->wlg", scaled_keys, value_rows, precision=peak_error)
    prior_state, kept_log = prefix_over_seq(block_state, last_state)
    prior_state = prior_state + jnp.exp(kept_log)[:, None, None] * carried_state
    output_rows = output_rows + jnp.exp(running_state)[:, :, None] * jnp.einsum(
        "ezy,eyl->ezl", query_rows, prior_state, precision=peak_error
    )
    normed_out = output_rows * lax.rsqrt(
        jnp.mean(output_rows * output_rows, axis=2, keepdims=True) + head_epsilon
    )
    branch = normed_out.transpose(1, 0, 2).reshape(span_rows, block_cols) * out_gain
    student_hidden = tok_cols + branch
    gap = student_hidden - teacher_hidden
    token_loss = over_copies(jnp.sum(gap * gap, axis=1), "expert") / width
    return (teacher_hidden.astype(BF16), student_hidden.astype(BF16), token_loss)


def solution(mesh):
    finer = Mesh(mesh.devices.reshape(8, 4, mesh.shape["expert"]), ("z", "x", "expert"))
    in_specs = (
        P(SEQ, None),
        P(),
        P(),
        P(SEQ, None),
        P("expert", None, SEQ),
        P("expert", None, SEQ),
        P("expert", SEQ, None),
        P(None, "expert"),
        P(None, "expert"),
        P("expert", SEQ),
        P("expert", None, None),
        P("expert"),
    )
    out_specs = (P(SEQ, "expert"), P(SEQ, "expert"), P(SEQ))
    return jax.shard_map(
        on_device, mesh=finer, in_specs=in_specs, out_specs=out_specs, check_vma=False
    )
```

```python
import functools

import jax
import jax.numpy as jnp
from jax import lax
from jax.experimental import pallas as pl
from jax.experimental.pallas import tpu as pltpu
from jax.sharding import Mesh
from jax.sharding import PartitionSpec as P

SEQ = ("z", "x")
ROWS_B = 16

norm_epsilon = 1e-05
head_epsilon = 1e-06
peak_error = lax.Precision.HIGHEST
F32 = jnp.float32
BF16 = jnp.bfloat16


def shift(value, axis, step, wrap=True):
    n = lax.axis_size(axis)
    pairs = [(i, (i + step) % n) for i in range(n) if wrap or 0 <= i + step < n]
    return lax.ppermute(value, axis, pairs)


def add(*terms):
    return sum(t.astype(F32) for t in terms).astype(BF16)


def mlp_kernel(n, steps, *refs):
    x_refs, (gate_ref, up_ref, down_ref) = refs[:n], refs[n : n + 3]
    out_refs = refs[n + 3 : 2 * n + 3]
    rest = refs[2 * n + 3 :]
    gates, ups, hiddens = rest[:n], rest[n : 2 * n], rest[2 * n :]
    i = pl.program_id(0)

    @pl.when(i == 0)
    def _():
        for k in range(n):
            gates[k][...] = jnp.zeros_like(gates[k])
            ups[k][...] = jnp.zeros_like(ups[k])

    @pl.when(i < steps)
    def _():
        for k in range(n):
            gates[k][...] += jnp.dot(x_refs[k][...], gate_ref[0], preferred_element_type=F32)
            ups[k][...] += jnp.dot(x_refs[k][...], up_ref[0], preferred_element_type=F32)

    @pl.when(i == steps - 1)
    def _():
        for k in range(n):
            v = gates[k][...]
            hiddens[k][...] = (v / (1.0 + jnp.exp(-v)) * ups[k][...]).astype(BF16)

    @pl.when(i >= steps)
    def _():
        for k in range(n):
            out_refs[k][...] = jnp.dot(
                hiddens[k][...], down_ref[0], preferred_element_type=F32
            ).astype(BF16)


def mlp(rows, gate, up, down):
    n = len(rows)
    width, hidden = gate.shape[1], gate.shape[2]
    steps = 8
    tile = width // steps
    first = lambda i: jnp.minimum(i, steps - 1)
    second = lambda i: jnp.maximum(i - steps, 0)
    total = sum(r.shape[0] for r in rows)
    return pl.pallas_call(
        functools.partial(mlp_kernel, n, steps),
        grid=(2 * steps,),
        in_specs=[pl.BlockSpec((r.shape[0], tile), lambda i: (0, first(i))) for r in rows]
        + [
            pl.BlockSpec((1, tile, hidden), lambda i: (0, first(i), 0)),
            pl.BlockSpec((1, tile, hidden), lambda i: (0, first(i), 0)),
            pl.BlockSpec((1, hidden, tile), lambda i: (0, 0, second(i))),
        ],
        out_specs=[pl.BlockSpec((r.shape[0], tile), lambda i: (0, second(i))) for r in rows],
        out_shape=[jax.ShapeDtypeStruct(r.shape, BF16) for r in rows],
        scratch_shapes=[pltpu.VMEM((r.shape[0], hidden), F32) for r in rows] * 2
        + [pltpu.VMEM((r.shape[0], hidden), BF16) for r in rows],
        compiler_params=pltpu.CompilerParams(vmem_limit_bytes=56 << 20),
        cost_estimate=pl.CostEstimate(
            flops=6 * total * width * hidden,
            bytes_accessed=4 * total * width + 6 * width * hidden,
            transcendentals=total * hidden,
        ),
    )(*rows, gate, up, down)


def route_kernel(mine_ref, tok_ref, gain_ref, router_ref, ids_ref, b_ref, a_ref, mix_ref, slot_ref):
    tok = tok_ref[...].astype(F32)
    scale = lax.rsqrt(jnp.mean(tok * tok, axis=1, keepdims=True) + norm_epsilon)
    normed = (tok * scale * gain_ref[...]).astype(BF16)
    contract = (((1,), (1,)), ((), ()))
    logits = lax.dot_general(router_ref[...], normed, contract, preferred_element_type=F32)
    experts, tokens = logits.shape
    expert = lax.broadcasted_iota(jnp.int32, logits.shape, 0)
    first, second = ids_ref[0:1, :] == expert, ids_ref[1:2, :] == expert
    chosen_first = jnp.sum(jnp.where(first, logits, 0.0), axis=0, keepdims=True)
    chosen_second = jnp.sum(jnp.where(second, logits, 0.0), axis=0, keepdims=True)
    share = 1.0 / (1.0 + jnp.exp(chosen_second - chosen_first))
    mix_ref[...] = jnp.where(first, share, 0.0) + jnp.where(second, 1.0 - share, 0.0)
    hits = first | second
    square = (tokens, tokens)
    earlier = lax.broadcasted_iota(jnp.int32, square, 0) < lax.broadcasted_iota(jnp.int32, square, 1)
    slots = jnp.dot(
        hits.astype(F32).astype(BF16), earlier.astype(F32).astype(BF16), preferred_element_type=F32
    ).astype(jnp.int32)
    slots = jnp.where(hits, slots, -1)
    slot_ref[...] = slots
    own = jnp.sum(jnp.where(expert == mine_ref[0], slots, 0), axis=0, keepdims=True)
    select = own == lax.broadcasted_iota(jnp.int32, (32, tokens), 0)
    rows = jnp.dot(
        select.astype(F32).astype(BF16), normed, preferred_element_type=F32
    ).astype(BF16)
    b_ref[...] = rows[: b_ref.shape[0]]
    a_ref[...] = rows[b_ref.shape[0] : b_ref.shape[0] + a_ref.shape[0]]


def route(mine, tokens, gain, router, ids, rows_b, rows_a):
    count, width = tokens.shape
    experts = router.shape[0]
    vmem = pl.BlockSpec(memory_space=pltpu.VMEM)
    return pl.pallas_call(
        route_kernel,
        in_specs=[pl.BlockSpec(memory_space=pltpu.SMEM)] + [vmem] * 4,
        out_specs=[vmem] * 4,
        out_shape=[
            jax.ShapeDtypeStruct((rows_b, width), BF16),
            jax.ShapeDtypeStruct((rows_a, width), BF16),
            jax.ShapeDtypeStruct((experts, count), F32),
            jax.ShapeDtypeStruct((experts, count), jnp.int32),
        ],
        compiler_params=pltpu.CompilerParams(vmem_limit_bytes=30 << 20),
    )(mine, tokens, gain, router, ids)


def stack_kernel(*refs):
    parts, out_ref, total = refs[:-2], refs[-2], refs[-1]
    rows = parts[0].shape[0]
    for k, part in enumerate(parts):
        total[k * rows : (k + 1) * rows, :] = part[...].astype(F32)
    out_ref[...] = total[...].astype(BF16)


def stack(parts):
    rows, width = parts[0].shape
    shape = (len(parts) * rows, width)
    vmem = pl.BlockSpec(memory_space=pltpu.VMEM)
    return pl.pallas_call(
        stack_kernel,
        in_specs=[vmem] * len(parts),
        out_specs=vmem,
        out_shape=jax.ShapeDtypeStruct(shape, BF16),
        scratch_shapes=[pltpu.VMEM(shape, F32)],
        compiler_params=pltpu.CompilerParams(vmem_limit_bytes=16 << 20),
    )(*parts)


def finish_kernel(offsets, *refs):
    own_a, parts_a = refs[0], refs[1:4]
    parts_b, out_ref = refs[4:-1], refs[-1]
    groups, rows, cols = out_ref.shape
    rows_b = parts_b[0].shape[0]
    rows_a = rows - rows_b
    for g in range(groups):
        span = slice(g * cols, (g + 1) * cols)
        b = sum(p[:, span].astype(F32) for p in parts_b)
        a = own_a[:, span].astype(F32)[:rows_a]
        for p, k in zip(parts_a, offsets):
            a = a + p[:, span].astype(F32)[k : k + rows_a]
        out_ref[g, :rows_b, :] = b.astype(BF16)
        out_ref[g, rows_b:, :] = a.astype(BF16)


def finish(own_a, parts_a, offsets, parts_b, groups, rows):
    width = own_a.shape[1]
    vmem = pl.BlockSpec(memory_space=pltpu.VMEM)
    return pl.pallas_call(
        functools.partial(finish_kernel, offsets),
        in_specs=[vmem] * (1 + len(parts_a) + len(parts_b)),
        out_specs=vmem,
        out_shape=jax.ShapeDtypeStruct((groups, rows, width // groups), BF16),
        compiler_params=pltpu.CompilerParams(vmem_limit_bytes=16 << 20),
    )(own_a, *parts_a, *parts_b)


def combine_kernel(arrived_ref, mix_ref, slot_ref, tok_ref, branch_ref, teach_ref, stud_ref, loss_ref):
    experts, rows, cols = arrived_ref.shape
    tokens = tok_ref.shape[0]
    place = lax.broadcasted_iota(jnp.int32, (rows, tokens), 0)
    contract = (((0,), (0,)), ((), ()))
    mixed = jnp.zeros((tokens, cols), F32)
    for e in range(experts):
        weigh = jnp.where(slot_ref[e : e + 1, :] == place, mix_ref[e : e + 1, :], 0.0)
        mixed = mixed + lax.dot_general(
            weigh,
            arrived_ref[e].astype(F32),
            contract,
            precision=peak_error,
            preferred_element_type=F32,
        )
    tok = tok_ref[...].astype(F32)
    teacher, student = tok + mixed, tok + branch_ref[...]
    teach_ref[...] = teacher.astype(BF16)
    stud_ref[...] = student.astype(BF16)
    gap = student - teacher
    loss_ref[...] = lax.dot_general(
        jnp.ones((experts, cols), F32),
        gap * gap,
        (((1,), (1,)), ((), ())),
        precision=peak_error,
        preferred_element_type=F32,
    )


def combine(arrived, mix, slots, tok_cols, branch):
    experts, _, cols = arrived.shape
    count = tok_cols.shape[0]
    vmem = pl.BlockSpec(memory_space=pltpu.VMEM)
    return pl.pallas_call(
        combine_kernel,
        in_specs=[vmem] * 5,
        out_specs=[vmem] * 3,
        out_shape=[
            jax.ShapeDtypeStruct((count, cols), BF16),
            jax.ShapeDtypeStruct((count, cols), BF16),
            jax.ShapeDtypeStruct((experts, count), F32),
        ],
        compiler_params=pltpu.CompilerParams(vmem_limit_bytes=16 << 20),
    )(arrived, mix, slots, tok_cols, branch)


def gather_z_by_hops(own):
    up1, down1 = shift(own, "z", 1), shift(own, "z", -1)
    up2, down2 = shift(up1, "z", 1), shift(down1, "z", -1)
    up3, down3 = shift(up2, "z", 1), shift(down2, "z", -1)
    up4 = shift(up3, "z", 1)
    return jnp.concatenate([own, up1, down1, up2, down2, up3, down3, up4])


def scatter_z_by_hops(parts):
    own, up1, down1, up2, down2, up3, down3, up4 = jnp.split(parts, 8)
    back = shift(up4, "z", -1)
    fore = shift(down3, "z", 1)
    back = shift(add(up3, back), "z", -1)
    fore = shift(add(down2, fore), "z", 1)
    back = shift(add(up2, back), "z", -1)
    fore = shift(add(down1, fore), "z", 1)
    back = shift(add(up1, back), "z", -1)
    return own, back, fore


def split_log(value):
    high = lax.reduce_precision(value, 8, 7)
    middle = lax.reduce_precision(value - high, 8, 7)
    return jnp.stack([high, middle, value - high - middle], axis=1)


def pack(state, log):
    heads, keys, size = state.shape
    logs = jnp.broadcast_to(split_log(log)[:, :, None], (heads, 3, size))
    logs = jnp.pad(logs, ((0, 0), (0, 13), (0, 0)))
    return jnp.concatenate([state, logs], axis=1).astype(BF16)


def unpack(packed):
    both = packed.astype(F32)
    return both[:, :-16], both[:, -16, 0] + both[:, -15, 0] + both[:, -14, 0]


def prefix_over_seq(state, log, after):
    x = lax.axis_index("x")
    packed, _ = lax.optimization_barrier((pack(state, log), after))
    parts = [unpack(packed)] + [unpack(shift(packed, "x", k)) for k in (1, 2, 3)]
    places = [lax.rem(x + 4 - k, 4) for k in range(4)]
    total_state = jnp.zeros_like(state)
    inside_state = jnp.zeros_like(state)
    inside_log = jnp.zeros_like(log)
    total_log = jnp.zeros_like(log)
    for k in range(4):
        after = jnp.zeros_like(log)
        within = jnp.zeros_like(log)
        for m in range(4):
            later = places[m] > places[k]
            after = after + jnp.where(later, parts[m][1], 0.0)
            within = within + jnp.where(later & (places[m] < x), parts[m][1], 0.0)
        total_state = total_state + jnp.exp(after)[:, None, None] * parts[k][0]
        total_log = total_log + parts[k][1]
        early = places[k] < x
        inside_state = inside_state + jnp.where(
            early, jnp.exp(within)[:, None, None] * parts[k][0], 0.0
        )
        inside_log = inside_log + jnp.where(early, parts[k][1], 0.0)
    run_packed = shift(pack(total_state, total_log), "z", 1, wrap=False)
    run_state, run_log = unpack(run_packed)
    for step in (1, 2, 4):
        before_state, before_log = unpack(shift(run_packed, "z", step, wrap=False))
        run_state = jnp.exp(run_log)[:, None, None] * before_state + run_state
        run_log = run_log + before_log
        if step < 4:
            run_packed = pack(run_state, run_log)
    state = jnp.exp(inside_log)[:, None, None] * run_state + inside_state
    return state, run_log + inside_log


def on_device(
    tokens,
    norm_gain,
    router_weight,
    expert_ids,
    gate_weight,
    up_weight,
    down_weight,
    query_weight,
    key_weight,
    log_decay,
    carried_state,
    out_gain,
):
    span_rows = tokens.shape[0]
    width = tokens.shape[1]
    expert_count = router_weight.shape[1]
    top_count = expert_ids.shape[1]
    capacity = 7 * top_count * span_rows // (8 * expert_count)
    groups = lax.axis_size("expert")
    mine = lax.axis_index("expert")
    block_cols = width // groups
    rows_a_count = capacity - ROWS_B
    own_b, own_a, mix_weight, slots = route(
        mine.reshape(1), tokens, norm_gain[None], router_weight.T, expert_ids.T, ROWS_B, rows_a_count
    )

    rows_b = gather_z_by_hops(own_b)
    rows_a = stack([own_a, shift(own_a, "x", 1), shift(own_a, "x", -1), shift(own_a, "x", 2)])
    rows_a = lax.all_gather(rows_a, "z", axis=0, tiled=True)
    half = rows_b.shape[0] // 2
    rows_p, rows_m = shift(rows_b, "x", 1), shift(rows_b, "x", -1)
    rows_o1, rows_o2 = shift(rows_p[:half], "x", 1), shift(rows_m[half:], "x", -1)
    late_tokens, _ = lax.optimization_barrier((tokens, rows_b))

    weights = (gate_weight, up_weight, down_weight)
    part_b, part_p, part_m = mlp([rows_b, rows_p, rows_m], *weights)
    part_o1, part_o2 = mlp([rows_o1, rows_o2], *weights)
    (part_a,) = mlp([rows_a], *weights)

    relay_p, relay_m = shift(part_o1, "x", -1), shift(part_o2, "x", 1)
    rest_p, rest_m = shift(part_p[half:], "x", -1), shift(part_m[:half], "x", 1)
    lead_p = shift(add(part_p[:half], relay_p), "x", -1)
    lead_m = shift(add(part_m[half:], relay_m), "x", 1)
    sum_b = jnp.concatenate(
        [add(part_b[:half], lead_p, rest_m), add(part_b[half:], rest_p, lead_m)]
    )
    terms_b = scatter_z_by_hops(sum_b)
    sum_a = lax.psum_scatter(part_a, "z", scatter_dimension=0, tiled=True)
    starts = [8 * (rows_a_count * k // 8) for k in (1, 2, 3)]
    offsets = [rows_a_count * k - at for k, at in zip((1, 2, 3), starts)]
    windows = [sum_a[at : at + 16] for at in starts]
    terms_a = [shift(w, "x", k) for w, k in zip(windows, (-1, 1, 2))]
    pieces = finish(sum_a, terms_a, offsets, terms_b, groups, capacity)
    arrived = lax.all_to_all(pieces, "expert", split_axis=0, concat_axis=0, tiled=True)

    tok_float = late_tokens.astype(F32)
    tok_cols = lax.dynamic_slice_in_dim(tok_float, mine * block_cols, block_cols, 1)
    heads_local = log_decay.shape[0]
    key_size = query_weight.shape[1] // heads_local
    head_size = block_cols // heads_local
    query_rows = (
        jnp.dot(late_tokens, query_weight, preferred_element_type=F32)
        .reshape(span_rows, heads_local, key_size)
        .transpose(1, 0, 2)
    )
    keys_proj = (
        jnp.dot(late_tokens, key_weight, preferred_element_type=F32)
        .reshape(span_rows, heads_local, key_size)
        .transpose(1, 0, 2)
    )
    value_rows = tok_cols.reshape(span_rows, heads_local, head_size).transpose(1, 0, 2)
    running_state = jnp.cumsum(log_decay, axis=1)
    last_state = running_state[:, -1]
    lower = jnp.arange(span_rows)[:, None] >= jnp.arange(span_rows)[None, :]
    gaps = running_state[:, :, None] - running_state[:, None, :]
    weights = jnp.where(lower[None], jnp.exp(jnp.minimum(gaps, 0.0)), 0.0)
    scores = jnp.einsum("htk,hsk->hts", query_rows, keys_proj, precision=peak_error) * weights
    output_rows = jnp.einsum("hts,hsv->htv", scores, value_rows, precision=peak_error)
    scaled_keys = keys_proj * jnp.exp(last_state[:, None] - running_state)[:, :, None]
    block_state = jnp.einsum("wpl,wpg->wlg", scaled_keys, value_rows, precision=peak_error)
    prior_state, kept_log = prefix_over_seq(block_state, last_state, rows_p)
    prior_state = prior_state + jnp.exp(kept_log)[:, None, None] * carried_state
    output_rows = output_rows + jnp.exp(running_state)[:, :, None] * jnp.einsum(
        "ezy,eyl->ezl", query_rows, prior_state, precision=peak_error
    )
    normed_out = output_rows * lax.rsqrt(
        jnp.mean(output_rows * output_rows, axis=2, keepdims=True) + head_epsilon
    )
    branch = normed_out.transpose(1, 0, 2).reshape(span_rows, block_cols) * out_gain
    teacher, student, loss = combine(
        arrived, mix_weight, slots, tok_cols.astype(BF16), branch
    )
    loss = lax.all_to_all(loss, "expert", split_axis=0, concat_axis=0, tiled=True)
    return teacher, student, jnp.sum(loss, axis=0) / width


def solution(mesh):
    finer = Mesh(mesh.devices.reshape(8, 4, mesh.shape["expert"]), ("z", "x", "expert"))
    in_specs = (
        P(SEQ, None),
        P(),
        P(),
        P(SEQ, None),
        P("expert", None, SEQ),
        P("expert", None, SEQ),
        P("expert", SEQ, None),
        P(None, "expert"),
        P(None, "expert"),
        P("expert", SEQ),
        P("expert", None, None),
        P("expert"),
    )
    out_specs = (P(SEQ, "expert"), P(SEQ, "expert"), P(SEQ))
    return jax.shard_map(
        on_device, mesh=finer, in_specs=in_specs, out_specs=out_specs, check_vma=False
    )
```

```python
import functools

import jax
import jax.numpy as jnp
from jax import lax
from jax.experimental import pallas as pl
from jax.experimental.pallas import tpu as pltpu
from jax.sharding import Mesh
from jax.sharding import PartitionSpec as P

SEQ = ("z", "x")
EXPERT = ("y", "core")

norm_epsilon = 1e-05
head_epsilon = 1e-06
peak_error = lax.Precision.HIGHEST
F32 = jnp.float32
BF16 = jnp.bfloat16


def shift(value, axis, step, wrap=True):
    n = lax.axis_size(axis)
    pairs = [(i, (i + step) % n) for i in range(n) if wrap or 0 <= i + step < n]
    return lax.ppermute(value, axis, pairs)


def hop(value, first=None, second=None):
    nz, nx = lax.axis_size("z"), lax.axis_size("x")
    pairs = []
    for z in range(nz):
        for x in range(nx):
            for core, way in enumerate((first, second)):
                if way is None:
                    continue
                axis, step = way
                to_z = (z + step) % nz if axis == "z" else z
                to_x = (x + step) % nx if axis == "x" else x
                pairs.append(((z * nx + x) * 2 + core, (to_z * nx + to_x) * 2 + core))
    return lax.ppermute(value, ("z", "x", "core"), pairs)


def add(*terms):
    return sum(t.astype(F32) for t in terms).astype(BF16)


def mlp_kernel(slots, tiles, core_ref, *refs):
    n_in = sum(len(s) for s in slots)
    n = len(slots)
    x_refs, (gate_hbm, up_hbm, down_hbm) = refs[:n_in], refs[n_in : n_in + 3]
    out_refs = refs[n_in + 3 : n_in + 3 + n]
    x, gate, up, down, out, gates, ups, hidden, x_sem, w_sem, d_sem, o_sem = refs[n_in + 3 + n :]
    rows = x.shape[0] // n
    tile = x.shape[1] // tiles
    core = core_ref[0]

    def weight_copies(t):
        span = pl.ds(t * tile, tile)
        return (
            pltpu.make_async_copy(gate_hbm.at[0, span], gate.at[span], w_sem.at[0, t]),
            pltpu.make_async_copy(up_hbm.at[0, span], up.at[span], w_sem.at[1, t]),
        )

    down_copy = pltpu.make_async_copy(down_hbm.at[0], down, d_sem)

    def for_rows(act):
        for k, choices in enumerate(slots):
            copies = [
                pltpu.make_async_copy(x_refs[j], x.at[pl.ds(k * rows, rows)], x_sem.at[k])
                for j in choices
            ]
            if len(copies) == 1:
                act(copies[0])
            else:
                for which, copy in enumerate(copies):
                    pl.when(core == which)(functools.partial(act, copy))

    for_rows(lambda copy: copy.start())
    for t in range(tiles):
        for copy in weight_copies(t):
            copy.start()
    down_copy.start()
    for_rows(lambda copy: copy.wait())
    gates[...] = jnp.zeros_like(gates)
    ups[...] = jnp.zeros_like(ups)

    @pl.loop(0, tiles)
    def _(t):
        for copy in weight_copies(t):
            copy.wait()
        span = pl.ds(pl.multiple_of(t * tile, tile), tile)
        gates[...] += jnp.dot(x[:, span], gate[span], preferred_element_type=F32)
        ups[...] += jnp.dot(x[:, span], up[span], preferred_element_type=F32)

    v = gates[...]
    hidden[...] = (v / (1.0 + jnp.exp(-v)) * ups[...]).astype(BF16)
    down_copy.wait()

    def out_copies(t):
        span = pl.ds(pl.multiple_of(t * tile, tile), tile)
        return [
            pltpu.make_async_copy(
                out.at[pl.ds(k * rows, rows), span], out_refs[k].at[:, span], o_sem.at[k, t]
            )
            for k in range(n)
        ]

    @pl.loop(0, tiles)
    def _(t):
        span = pl.ds(pl.multiple_of(t * tile, tile), tile)
        out[:, span] = jnp.dot(hidden[...], down[:, span], preferred_element_type=F32).astype(BF16)
        for copy in out_copies(t):
            copy.start()

    @pl.loop(0, tiles)
    def _(t):
        for copy in out_copies(t):
            copy.wait()


def mlp(core, slots, gate, up, down):
    arrays = [a for slot in slots for a in slot]
    where, at = [], 0
    for slot in slots:
        where.append(tuple(range(at, at + len(slot))))
        at += len(slot)
    n, tiles = len(slots), 4
    rows, width = arrays[0].shape
    hidden = gate.shape[2]
    total = n * rows
    anywhere = pl.BlockSpec(memory_space=pl.ANY)
    return pl.pallas_call(
        functools.partial(mlp_kernel, tuple(where), tiles),
        in_specs=[pl.BlockSpec(memory_space=pltpu.SMEM)] + [anywhere] * (len(arrays) + 3),
        out_specs=[anywhere] * n,
        out_shape=[jax.ShapeDtypeStruct((rows, width), BF16)] * n,
        scratch_shapes=[
            pltpu.VMEM((total, width), BF16),
            pltpu.VMEM((width, hidden), BF16),
            pltpu.VMEM((width, hidden), BF16),
            pltpu.VMEM((hidden, width), BF16),
            pltpu.VMEM((total, width), BF16),
            pltpu.VMEM((total, hidden), F32),
            pltpu.VMEM((total, hidden), F32),
            pltpu.VMEM((total, hidden), BF16),
            pltpu.SemaphoreType.DMA((n,)),
            pltpu.SemaphoreType.DMA((2, tiles)),
            pltpu.SemaphoreType.DMA,
            pltpu.SemaphoreType.DMA((n, tiles)),
        ],
        compiler_params=pltpu.CompilerParams(vmem_limit_bytes=56 << 20),
        cost_estimate=pl.CostEstimate(
            flops=6 * total * width * hidden,
            bytes_accessed=4 * total * width + 6 * width * hidden,
            transcendentals=total * hidden,
        ),
    )(core, *arrays, gate, up, down)


def route_kernel(mine_ref, tok_ref, gain_ref, router_ref, ids_ref, rows_ref, mix_ref, slot_ref):
    tok = tok_ref[...].astype(F32)
    scale = lax.rsqrt(jnp.mean(tok * tok, axis=1, keepdims=True) + norm_epsilon)
    normed = (tok * scale * gain_ref[...]).astype(BF16)
    contract = (((1,), (1,)), ((), ()))
    logits = lax.dot_general(router_ref[...], normed, contract, preferred_element_type=F32)
    experts, tokens = logits.shape
    expert = lax.broadcasted_iota(jnp.int32, logits.shape, 0)
    first, second = ids_ref[0:1, :] == expert, ids_ref[1:2, :] == expert
    chosen_first = jnp.sum(jnp.where(first, logits, 0.0), axis=0, keepdims=True)
    chosen_second = jnp.sum(jnp.where(second, logits, 0.0), axis=0, keepdims=True)
    share = 1.0 / (1.0 + jnp.exp(chosen_second - chosen_first))
    mix_ref[...] = jnp.where(first, share, 0.0) + jnp.where(second, 1.0 - share, 0.0)
    hits = first | second
    square = (tokens, tokens)
    earlier = lax.broadcasted_iota(jnp.int32, square, 0) < lax.broadcasted_iota(jnp.int32, square, 1)
    slots = jnp.dot(
        hits.astype(F32).astype(BF16), earlier.astype(F32).astype(BF16), preferred_element_type=F32
    ).astype(jnp.int32)
    slots = jnp.where(hits, slots, -1)
    slot_ref[...] = slots
    own = jnp.sum(jnp.where(expert == mine_ref[0], slots, 0), axis=0, keepdims=True)
    select = own == lax.broadcasted_iota(jnp.int32, (32, tokens), 0)
    rows = jnp.dot(select.astype(F32).astype(BF16), normed, preferred_element_type=F32)
    rows_ref[...] = rows.astype(BF16)[: rows_ref.shape[0]]


def route(mine, tokens, gain, router, ids, rows):
    count, width = tokens.shape
    experts = router.shape[0]
    vmem = pl.BlockSpec(memory_space=pltpu.VMEM)
    return pl.pallas_call(
        route_kernel,
        in_specs=[pl.BlockSpec(memory_space=pltpu.SMEM)] + [vmem] * 4,
        out_specs=[vmem] * 3,
        out_shape=[
            jax.ShapeDtypeStruct((rows, width), BF16),
            jax.ShapeDtypeStruct((experts, count), F32),
            jax.ShapeDtypeStruct((experts, count), jnp.int32),
        ],
        compiler_params=pltpu.CompilerParams(vmem_limit_bytes=30 << 20),
    )(mine, tokens, gain, router, ids)


def stack_kernel(core_ref, *refs):
    parts, other, out_ref, total = refs[:-3], refs[-3], refs[-2], refs[-1]
    rows = parts[0].shape[0]

    @pl.when(core_ref[0] == 1)
    def _():
        for k, part in enumerate(parts):
            total[k * rows : (k + 1) * rows, :] = part[...].astype(F32)
        out_ref[...] = total[...].astype(BF16)

    @pl.when(core_ref[0] == 0)
    def _():
        out_ref[...] = other[...]


def stack_all_kernel(*refs):
    parts, out_ref, total = refs[:-2], refs[-2], refs[-1]
    rows = parts[0].shape[0]
    for k, part in enumerate(parts):
        total[k * rows : (k + 1) * rows, :] = part[...].astype(F32)
    out_ref[...] = total[...].astype(BF16)


def stack(parts, core=None, other=None):
    rows, width = parts[0].shape
    shape = (len(parts) * rows, width)
    vmem = pl.BlockSpec(memory_space=pltpu.VMEM)
    smem = pl.BlockSpec(memory_space=pltpu.SMEM)
    args = list(parts) if other is None else [core, *parts, other]
    return pl.pallas_call(
        stack_all_kernel if other is None else stack_kernel,
        in_specs=[vmem] * len(parts) if other is None else [smem] + [vmem] * (len(parts) + 1),
        out_specs=vmem,
        out_shape=jax.ShapeDtypeStruct(shape, BF16),
        scratch_shapes=[pltpu.VMEM(shape, F32)],
        compiler_params=pltpu.CompilerParams(vmem_limit_bytes=16 << 20),
    )(*args)


def finish_kernel(offsets, *refs):
    parts, out_ref = refs[:-1], refs[-1]
    groups, rows, cols = out_ref.shape
    for g in range(groups):
        span = slice(g * cols, (g + 1) * cols)
        out_ref[g, :, :] = sum(
            p[:, span].astype(F32)[k : k + rows] for p, k in zip(parts, offsets)
        ).astype(BF16)


def finish(parts, offsets, groups, rows):
    width = parts[0].shape[1]
    vmem = pl.BlockSpec(memory_space=pltpu.VMEM)
    return pl.pallas_call(
        functools.partial(finish_kernel, offsets),
        in_specs=[vmem] * len(parts),
        out_specs=vmem,
        out_shape=jax.ShapeDtypeStruct((groups, rows, width // groups), BF16),
        compiler_params=pltpu.CompilerParams(vmem_limit_bytes=16 << 20),
    )(*parts)


def combine_kernel(arrived_ref, mix_ref, slot_ref, tok_ref, branch_ref, teach_ref, stud_ref, loss_ref):
    experts, rows, cols = arrived_ref.shape
    tokens = tok_ref.shape[0]
    place = lax.broadcasted_iota(jnp.int32, (rows, tokens), 0)
    contract = (((0,), (0,)), ((), ()))
    mixed = jnp.zeros((tokens, cols), F32)
    for e in range(experts):
        weigh = jnp.where(slot_ref[e : e + 1, :] == place, mix_ref[e : e + 1, :], 0.0)
        mixed = mixed + lax.dot_general(
            weigh,
            arrived_ref[e].astype(F32),
            contract,
            precision=peak_error,
            preferred_element_type=F32,
        )
    tok = tok_ref[...].astype(F32)
    teacher, student = tok + mixed, tok + branch_ref[...]
    teach_ref[...] = teacher.astype(BF16)
    stud_ref[...] = student.astype(BF16)
    gap = student - teacher
    loss_ref[...] = lax.dot_general(
        jnp.ones((experts, cols), F32),
        gap * gap,
        (((1,), (1,)), ((), ())),
        precision=peak_error,
        preferred_element_type=F32,
    )


def combine(arrived, mix, slots, tok_cols, branch):
    experts, _, cols = arrived.shape
    count = tok_cols.shape[0]
    vmem = pl.BlockSpec(memory_space=pltpu.VMEM)
    return pl.pallas_call(
        combine_kernel,
        in_specs=[vmem] * 5,
        out_specs=[vmem] * 3,
        out_shape=[
            jax.ShapeDtypeStruct((count, cols), BF16),
            jax.ShapeDtypeStruct((count, cols), BF16),
            jax.ShapeDtypeStruct((experts, count), F32),
        ],
        compiler_params=pltpu.CompilerParams(vmem_limit_bytes=16 << 20),
    )(arrived, mix, slots, tok_cols, branch)


def split_log(value):
    high = lax.reduce_precision(value, 8, 7)
    middle = lax.reduce_precision(value - high, 8, 7)
    return jnp.stack([high, middle, value - high - middle], axis=1)


def pack(state, log):
    heads, keys, size = state.shape
    logs = jnp.broadcast_to(split_log(log)[:, :, None], (heads, 3, size))
    logs = jnp.pad(logs, ((0, 0), (0, 13), (0, 0)))
    return jnp.concatenate([state, logs], axis=1).astype(BF16)


def unpack(packed):
    both = packed.astype(F32)
    return both[:, :-16], both[:, -16, 0] + both[:, -15, 0] + both[:, -14, 0]


def prefix_over_seq(state, log, after):
    x = lax.axis_index("x")
    packed, _ = lax.optimization_barrier((pack(state, log), after))
    parts = [unpack(packed)] + [unpack(shift(packed, "x", k)) for k in (1, 2, 3)]
    places = [lax.rem(x + 4 - k, 4) for k in range(4)]
    total_state = jnp.zeros_like(state)
    inside_state = jnp.zeros_like(state)
    inside_log = jnp.zeros_like(log)
    total_log = jnp.zeros_like(log)
    for k in range(4):
        after = jnp.zeros_like(log)
        within = jnp.zeros_like(log)
        for m in range(4):
            later = places[m] > places[k]
            after = after + jnp.where(later, parts[m][1], 0.0)
            within = within + jnp.where(later & (places[m] < x), parts[m][1], 0.0)
        total_state = total_state + jnp.exp(after)[:, None, None] * parts[k][0]
        total_log = total_log + parts[k][1]
        early = places[k] < x
        inside_state = inside_state + jnp.where(
            early, jnp.exp(within)[:, None, None] * parts[k][0], 0.0
        )
        inside_log = inside_log + jnp.where(early, parts[k][1], 0.0)
    run_packed = shift(pack(total_state, total_log), "z", 1, wrap=False)
    run_state, run_log = unpack(run_packed)
    for step in (1, 2, 4):
        before_state, before_log = unpack(shift(run_packed, "z", step, wrap=False))
        run_state = jnp.exp(run_log)[:, None, None] * before_state + run_state
        run_log = run_log + before_log
        if step < 4:
            run_packed = pack(run_state, run_log)
    state = jnp.exp(inside_log)[:, None, None] * run_state + inside_state
    return state, run_log + inside_log


def on_device(
    tokens,
    norm_gain,
    router_weight,
    expert_ids,
    gate_weight,
    up_weight,
    down_weight,
    query_weight,
    key_weight,
    log_decay,
    carried_state,
    out_gain,
):
    span_rows = tokens.shape[0]
    width = tokens.shape[1]
    expert_count = router_weight.shape[1]
    top_count = expert_ids.shape[1]
    capacity = 7 * top_count * span_rows // (8 * expert_count)
    groups = lax.axis_size(EXPERT)
    mine = lax.axis_index(EXPERT)
    block_cols = width // groups
    core_index = lax.axis_index("core")
    core = core_index.reshape(1)
    is_first = core_index == 0
    own, mix_weight, slots = route(
        mine.reshape(1), tokens, norm_gain[None], router_weight.T, expert_ids.T, capacity
    )

    up, down = ("z", 1), ("z", -1)
    right, left = ("x", 1), ("x", -1)
    near_u, near_d = hop(own, right, up), hop(own, left, down)
    next_u, next_d = hop(near_u, right, up), hop(near_d, None, down)
    third_u, third_d = hop(next_u, None, up), hop(next_d, None, down)
    fourth_u = hop(third_u, None, up)
    lead = stack([own, near_u, near_d, next_u])
    u0, d0 = hop(lead, up, ("x", 0)), hop(lead, down)
    d0 = stack([next_d, third_u, third_d, fourth_u], core, d0)
    u1, d1 = hop(u0, up, right), hop(d0, down, left)
    u2, d2 = hop(u1, up, right), hop(d1, down, left)
    u3 = hop(u2, up)
    side_u, side_d = hop(d0, None, right), hop(lead, None, left)

    weights = (gate_weight, up_weight, down_weight)
    part_u0, part_d0, part_u1, part_d1 = mlp(core, [(u0,), (d0,), (u1,), (d1,)], *weights)
    part_u2, part_d2 = mlp(core, [(u2,), (d2,)], *weights)
    part_6, part_7 = mlp(core, [(lead, side_d), (u3, side_u)], *weights)

    last_u = hop(part_7, down, left)
    side_u = jnp.where(is_first, 0.0, last_u.astype(F32))
    side_d = hop(part_6, None, right)
    back = hop(add(part_u2, jnp.where(is_first, last_u.astype(F32), 0.0)), down, left)
    fore = hop(part_d2, up, right)
    back = hop(add(part_u1, back), down, left)
    fore = hop(add(part_d1, fore), up, right)
    far = add(part_d0, fore, side_u)
    home_u = hop(add(part_u0, back), down)
    home_d = hop(far, up)
    near = jnp.where(
        is_first,
        part_6.astype(F32) + home_u.astype(F32) + home_d.astype(F32),
        part_u0.astype(F32) + back.astype(F32) + side_d.astype(F32),
    ).astype(BF16)
    spots = [(8 * (capacity * k // 8), capacity * k % 8) for k in range(4)]
    far_ways = (("z", 2), ("z", -3), ("z", 3), ("z", 4))
    near_ways = (None, (left, down), (right, up), (("x", 2), ("z", -2)))
    parts = [near[:32]]
    for (at, _), ways in zip(spots[1:], near_ways[1:]):
        parts.append(hop(near[at : at + 32], *ways))
    for (at, _), way in zip(spots, far_ways):
        parts.append(hop(far[at : at + 32], None, way))
    offsets = [off for _, off in spots] + [off for _, off in spots]
    pieces = finish(parts, tuple(offsets), groups, capacity)
    arrived = lax.all_to_all(pieces, EXPERT, split_axis=0, concat_axis=0, tiled=True)
    late_tokens = tokens

    tok_float = late_tokens.astype(F32)
    tok_cols = lax.dynamic_slice_in_dim(tok_float, mine * block_cols, block_cols, 1)
    heads_local = log_decay.shape[0]
    key_size = query_weight.shape[1] // heads_local
    head_size = block_cols // heads_local
    query_rows = (
        jnp.dot(late_tokens, query_weight, preferred_element_type=F32)
        .reshape(span_rows, heads_local, key_size)
        .transpose(1, 0, 2)
    )
    keys_proj = (
        jnp.dot(late_tokens, key_weight, preferred_element_type=F32)
        .reshape(span_rows, heads_local, key_size)
        .transpose(1, 0, 2)
    )
    value_rows = tok_cols.reshape(span_rows, heads_local, head_size).transpose(1, 0, 2)
    running_state = jnp.cumsum(log_decay, axis=1)
    last_state = running_state[:, -1]
    lower = jnp.arange(span_rows)[:, None] >= jnp.arange(span_rows)[None, :]
    gaps = running_state[:, :, None] - running_state[:, None, :]
    weights = jnp.where(lower[None], jnp.exp(jnp.minimum(gaps, 0.0)), 0.0)
    scores = jnp.einsum("htk,hsk->hts", query_rows, keys_proj, precision=peak_error) * weights
    output_rows = jnp.einsum("hts,hsv->htv", scores, value_rows, precision=peak_error)
    scaled_keys = keys_proj * jnp.exp(last_state[:, None] - running_state)[:, :, None]
    block_state = jnp.einsum("wpl,wpg->wlg", scaled_keys, value_rows, precision=peak_error)
    prior_state, kept_log = prefix_over_seq(block_state, last_state, u1)
    prior_state = prior_state + jnp.exp(kept_log)[:, None, None] * carried_state
    output_rows = output_rows + jnp.exp(running_state)[:, :, None] * jnp.einsum(
        "ezy,eyl->ezl", query_rows, prior_state, precision=peak_error
    )
    normed_out = output_rows * lax.rsqrt(
        jnp.mean(output_rows * output_rows, axis=2, keepdims=True) + head_epsilon
    )
    branch = normed_out.transpose(1, 0, 2).reshape(span_rows, block_cols) * out_gain
    teacher, student, loss = combine(
        arrived, mix_weight, slots, tok_cols.astype(BF16), branch
    )
    loss = lax.all_to_all(loss, EXPERT, split_axis=0, concat_axis=0, tiled=True)
    return teacher, student, jnp.sum(loss, axis=0) / width


def solution(mesh):
    finer = Mesh(mesh.devices.reshape(8, 4, 4, 2), ("z", "x", "y", "core"))
    in_specs = (
        P(SEQ, None),
        P(),
        P(),
        P(SEQ, None),
        P(EXPERT, None, SEQ),
        P(EXPERT, None, SEQ),
        P(EXPERT, SEQ, None),
        P(None, EXPERT),
        P(None, EXPERT),
        P(EXPERT, SEQ),
        P(EXPERT, None, None),
        P(EXPERT),
    )
    out_specs = (P(SEQ, EXPERT), P(SEQ, EXPERT), P(SEQ))
    return jax.shard_map(
        on_device, mesh=finer, in_specs=in_specs, out_specs=out_specs, check_vma=False
    )
```

```python
import functools

import jax
import jax.numpy as jnp
from jax import lax
from jax.experimental import pallas as pl
from jax.experimental.pallas import tpu as pltpu
from jax.sharding import Mesh
from jax.sharding import PartitionSpec as P

SEQ = ("z", "x")
EXPERT = ("y", "core")
ROWS_A = 14

norm_epsilon = 1e-05
head_epsilon = 1e-06
peak_error = lax.Precision.HIGHEST
F32 = jnp.float32
BF16 = jnp.bfloat16


def shift(value, axis, step, wrap=True):
    n = lax.axis_size(axis)
    pairs = [(i, (i + step) % n) for i in range(n) if wrap or 0 <= i + step < n]
    return lax.ppermute(value, axis, pairs)


def add(*terms):
    return sum(t.astype(F32) for t in terms).astype(BF16)


def mlp_kernel(n_in, n_out, tiles, *refs):
    x_refs, (gate_hbm, up_hbm, down_hbm) = refs[:n_in], refs[n_in : n_in + 3]
    out_refs = refs[n_in + 3 : n_in + 3 + n_out]
    scratch = refs[n_in + 3 + n_out :]
    x, gate, up, down, out, gates, ups, hidden, x_sem, w_sem, d_sem, o_sem = scratch
    tile = x.shape[1] // tiles

    def span_of(t):
        return pl.ds(pl.multiple_of(t * tile, tile), tile)

    def weight_copies(t):
        span = span_of(t)
        return (
            pltpu.make_async_copy(gate_hbm.at[0, span], gate.at[span], w_sem.at[0, t]),
            pltpu.make_async_copy(up_hbm.at[0, span], up.at[span], w_sem.at[1, t]),
        )

    def for_rows(t, act):
        span = span_of(t)
        at = 0
        for k, ref in enumerate(x_refs):
            size = ref.shape[0]
            act(
                pltpu.make_async_copy(
                    ref.at[:, span], x.at[pl.ds(at, size), span], x_sem.at[k, t]
                )
            )
            at += size

    down_copy = pltpu.make_async_copy(down_hbm.at[0], down, d_sem)

    @pl.loop(0, tiles)
    def _(t):
        for copy in weight_copies(t):
            copy.start()
        for_rows(t, lambda copy: copy.start())

    down_copy.start()
    gates[...] = jnp.zeros_like(gates)
    ups[...] = jnp.zeros_like(ups)

    @pl.loop(0, tiles)
    def _(t):
        for copy in weight_copies(t):
            copy.wait()
        for_rows(t, lambda copy: copy.wait())
        span = span_of(t)
        gates[...] += jnp.dot(x[:, span], gate[span], preferred_element_type=F32)
        ups[...] += jnp.dot(x[:, span], up[span], preferred_element_type=F32)

    v = gates[...]
    hidden[...] = (v / (1.0 + jnp.exp(-v)) * ups[...]).astype(BF16)
    down_copy.wait()

    def out_copies(t):
        span = span_of(t)
        at, copies = 0, []
        for k, ref in enumerate(out_refs):
            size = ref.shape[0]
            copies.append(
                pltpu.make_async_copy(
                    out.at[pl.ds(at, size), span], ref.at[:, span], o_sem.at[k, t]
                )
            )
            at += size
        return copies

    @pl.loop(0, tiles)
    def _(t):
        span = span_of(t)
        out[:, span] = jnp.dot(hidden[...], down[:, span], preferred_element_type=F32).astype(BF16)
        for copy in out_copies(t):
            copy.start()

    @pl.loop(0, tiles)
    def _(t):
        for copy in out_copies(t):
            copy.wait()


def mlp(arrays, sizes, gate, up, down):
    tiles, width, hidden = 4, gate.shape[1], gate.shape[2]
    total = sum(sizes)
    anywhere = pl.BlockSpec(memory_space=pltpu.MemorySpace.HBM)
    return pl.pallas_call(
        functools.partial(mlp_kernel, len(arrays), len(sizes), tiles),
        in_specs=[anywhere] * (len(arrays) + 3),
        out_specs=[anywhere] * len(sizes),
        out_shape=[jax.ShapeDtypeStruct((n, width), BF16) for n in sizes],
        scratch_shapes=[
            pltpu.VMEM((total, width), BF16),
            pltpu.VMEM((width, hidden), BF16),
            pltpu.VMEM((width, hidden), BF16),
            pltpu.VMEM((hidden, width), BF16),
            pltpu.VMEM((total, width), BF16),
            pltpu.VMEM((total, hidden), F32),
            pltpu.VMEM((total, hidden), F32),
            pltpu.VMEM((total, hidden), BF16),
            pltpu.SemaphoreType.DMA((len(arrays), tiles)),
            pltpu.SemaphoreType.DMA((2, tiles)),
            pltpu.SemaphoreType.DMA,
            pltpu.SemaphoreType.DMA((len(sizes), tiles)),
        ],
        compiler_params=pltpu.CompilerParams(vmem_limit_bytes=56 << 20),
        cost_estimate=pl.CostEstimate(
            flops=6 * total * width * hidden,
            bytes_accessed=4 * total * width + 6 * width * hidden,
            transcendentals=total * hidden,
        ),
    )(*arrays, gate, up, down)


def route_kernel(mine_ref, *refs):
    given, (a_ref, b_ref, mix_ref, slot_ref), held, sems = refs[:4], refs[4:8], refs[8:12], refs[12]
    copies = [pltpu.make_async_copy(g, h, sems.at[k]) for k, (g, h) in enumerate(zip(given, held))]
    for copy in copies:
        copy.start()
    for copy in copies:
        copy.wait()
    tok_ref, gain_ref, router_ref, ids_ref = held
    tok = tok_ref[...].astype(F32)
    scale = lax.rsqrt(jnp.mean(tok * tok, axis=1, keepdims=True) + norm_epsilon)
    normed = (tok * scale * gain_ref[...]).astype(BF16)
    contract = (((1,), (1,)), ((), ()))
    logits = lax.dot_general(router_ref[...], normed, contract, preferred_element_type=F32)
    experts, tokens = logits.shape
    expert = lax.broadcasted_iota(jnp.int32, logits.shape, 0)
    first, second = ids_ref[0:1, :] == expert, ids_ref[1:2, :] == expert
    chosen_first = jnp.sum(jnp.where(first, logits, 0.0), axis=0, keepdims=True)
    chosen_second = jnp.sum(jnp.where(second, logits, 0.0), axis=0, keepdims=True)
    share = 1.0 / (1.0 + jnp.exp(chosen_second - chosen_first))
    mix_ref[...] = jnp.where(first, share, 0.0) + jnp.where(second, 1.0 - share, 0.0)
    hits = first | second
    square = (tokens, tokens)
    earlier = lax.broadcasted_iota(jnp.int32, square, 0) < lax.broadcasted_iota(jnp.int32, square, 1)
    slots = jnp.dot(
        hits.astype(F32).astype(BF16), earlier.astype(F32).astype(BF16), preferred_element_type=F32
    ).astype(jnp.int32)
    slots = jnp.where(hits, slots, -1)
    slot_ref[...] = slots
    own = jnp.sum(jnp.where(expert == mine_ref[0], slots, 0), axis=0, keepdims=True)
    place = lax.broadcasted_iota(jnp.int32, (16, tokens), 0)
    for ref, start in ((a_ref, 0), (b_ref, a_ref.shape[0])):
        select = (own == place + start).astype(F32).astype(BF16)
        rows = jnp.dot(select, normed, preferred_element_type=F32).astype(BF16)
        ref[...] = rows[: ref.shape[0]]


def route(mine, tokens, gain, router, ids, rows_a, rows_b):
    count, width = tokens.shape
    experts = router.shape[0]
    vmem = pl.BlockSpec(memory_space=pltpu.VMEM)
    return pl.pallas_call(
        route_kernel,
        in_specs=[pl.BlockSpec(memory_space=pltpu.SMEM)]
        + [pl.BlockSpec(memory_space=pltpu.MemorySpace.HBM)] * 4,
        out_specs=[vmem] * 4,
        out_shape=[
            jax.ShapeDtypeStruct((rows_a, width), BF16),
            jax.ShapeDtypeStruct((rows_b, width), BF16),
            jax.ShapeDtypeStruct((experts, count), F32),
            jax.ShapeDtypeStruct((experts, count), jnp.int32),
        ],
        scratch_shapes=[pltpu.VMEM(v.shape, v.dtype) for v in (tokens, gain, router, ids)]
        + [pltpu.SemaphoreType.DMA((4,))],
        compiler_params=pltpu.CompilerParams(vmem_limit_bytes=58 << 20),
    )(mine, tokens, gain, router, ids)


def staged_kernel(kernel, scalars, count, *refs):
    given, rest = refs[scalars : scalars + count], refs[scalars + count :]
    held, sems = rest[-count - 1 : -1], rest[-1]
    copies = [pltpu.make_async_copy(g, h, sems.at[k]) for k, (g, h) in enumerate(zip(given, held))]
    for copy in copies:
        copy.start()
    for copy in copies:
        copy.wait()
    kernel(*refs[:scalars], *held, *rest[: -count - 1])


def small_call(kernel, out_shape, *args, scalars=0, scratch=()):
    arrays = args[scalars:]
    return pl.pallas_call(
        functools.partial(staged_kernel, kernel, scalars, len(arrays)),
        in_specs=[pl.BlockSpec(memory_space=pltpu.SMEM)] * scalars
        + [pl.BlockSpec(memory_space=pl.ANY)] * len(arrays),
        out_specs=jax.tree.map(lambda _: pl.BlockSpec(memory_space=pltpu.VMEM), out_shape),
        out_shape=out_shape,
        scratch_shapes=list(scratch)
        + [pltpu.VMEM(v.shape, v.dtype) for v in arrays]
        + [pltpu.SemaphoreType.DMA((len(arrays),))],
        compiler_params=pltpu.CompilerParams(vmem_limit_bytes=58 << 20),
    )(*args)


def stack_kernel(*refs):
    parts, out_ref, total = refs[:-2], refs[-2], refs[-1]
    rows = parts[0].shape[0]
    for k, part in enumerate(parts):
        total[k * rows : (k + 1) * rows, :] = part[...].astype(F32)
    out_ref[...] = total[...].astype(BF16)


def stack(parts):
    rows, width = parts[0].shape
    shape = (len(parts) * rows, width)
    return small_call(
        stack_kernel, jax.ShapeDtypeStruct(shape, BF16), *parts, scratch=[pltpu.VMEM(shape, F32)]
    )


def rows_from(ref, at, rows):
    low, high = at // 8 * 8, min(-(-(at + rows) // 8) * 8, ref.shape[0])
    return ref[low:high, :].astype(F32)[at - low : at - low + rows]


def pick_kernel(ats, summed, value_ref, *refs):
    terms, outs = refs[:summed], refs[summed:]
    for k, (at, out) in enumerate(zip(ats, outs)):
        rows = rows_from(value_ref, at, out.shape[0])
        if summed:
            rows = rows + terms[k][...].astype(F32)
        out[...] = rows.astype(BF16)


def pick(value, ats, rows, terms=()):
    vmem = pl.BlockSpec(memory_space=pltpu.VMEM)
    return pl.pallas_call(
        functools.partial(pick_kernel, ats, len(terms)),
        in_specs=[vmem] * (1 + len(terms)),
        out_specs=[vmem] * len(ats),
        out_shape=[jax.ShapeDtypeStruct((rows, value.shape[1]), BF16)] * len(ats),
        compiler_params=pltpu.CompilerParams(vmem_limit_bytes=16 << 20),
    )(value, *terms)


def finish_kernel(n_a, *refs):
    parts_a, parts_b, out_ref, total = refs[:n_a], refs[n_a:-2], refs[-2], refs[-1]
    groups, rows, cols = out_ref.shape
    rows_a = parts_a[1].shape[0]
    total[:rows_a, :] = sum(rows_from(p, 0, rows_a) for p in parts_a)
    total[rows_a:rows, :] = sum(rows_from(p, 0, rows - rows_a) for p in parts_b)
    for g in range(groups):
        out_ref[g, :, :] = total[:rows, g * cols : (g + 1) * cols].astype(BF16)


def finish(parts_a, parts_b, groups, rows):
    width = parts_a[0].shape[1]
    vmem = pl.BlockSpec(memory_space=pltpu.VMEM)
    return pl.pallas_call(
        functools.partial(finish_kernel, len(parts_a)),
        in_specs=[vmem] * (len(parts_a) + len(parts_b)),
        out_specs=vmem,
        out_shape=jax.ShapeDtypeStruct((groups, rows, width // groups), BF16),
        scratch_shapes=[pltpu.VMEM((32, width), F32)],
        compiler_params=pltpu.CompilerParams(vmem_limit_bytes=16 << 20),
    )(*parts_a, *parts_b)


def combine_kernel(arrived_ref, mix_ref, slot_ref, tok_ref, branch_ref, teach_ref, stud_ref, loss_ref):
    experts, rows, cols = arrived_ref.shape
    tokens = tok_ref.shape[0]
    place = lax.broadcasted_iota(jnp.int32, (rows, tokens), 0)
    contract = (((0,), (0,)), ((), ()))
    mixed = jnp.zeros((tokens, cols), F32)
    for e in range(experts):
        weigh = jnp.where(slot_ref[e : e + 1, :] == place, mix_ref[e : e + 1, :], 0.0)
        mixed = mixed + lax.dot_general(
            weigh,
            arrived_ref[e].astype(F32),
            contract,
            precision=peak_error,
            preferred_element_type=F32,
        )
    tok = tok_ref[...].astype(F32)
    teacher, student = tok + mixed, tok + branch_ref[...]
    teach_ref[...] = teacher.astype(BF16)
    stud_ref[...] = student.astype(BF16)
    gap = student - teacher
    loss_ref[...] = lax.dot_general(
        jnp.ones((experts, cols), F32),
        gap * gap,
        (((1,), (1,)), ((), ())),
        precision=peak_error,
        preferred_element_type=F32,
    )


def combine(arrived, mix, slots, tok_cols, branch):
    experts, _, cols = arrived.shape
    count = tok_cols.shape[0]
    vmem = pl.BlockSpec(memory_space=pltpu.VMEM)
    return pl.pallas_call(
        combine_kernel,
        in_specs=[vmem] * 5,
        out_specs=[vmem] * 3,
        out_shape=[
            jax.ShapeDtypeStruct((count, cols), BF16),
            jax.ShapeDtypeStruct((count, cols), BF16),
            jax.ShapeDtypeStruct((experts, count), F32),
        ],
        compiler_params=pltpu.CompilerParams(vmem_limit_bytes=16 << 20),
    )(arrived, mix, slots, tok_cols, branch)


def split_log(value):
    high = lax.reduce_precision(value, 8, 7)
    middle = lax.reduce_precision(value - high, 8, 7)
    return jnp.stack([high, middle, value - high - middle], axis=1)


def pack(state, log):
    heads, keys, size = state.shape
    logs = jnp.broadcast_to(split_log(log)[:, :, None], (heads, 3, size))
    logs = jnp.pad(logs, ((0, 0), (0, 13), (0, 0)))
    return jnp.concatenate([state, logs], axis=1).astype(BF16)


def read_packed(ref, h):
    size = ref.shape[1] - 16
    logs = ref[h, size : size + 16, :].astype(F32)
    return ref[h, :size, :].astype(F32), logs[0:1] + logs[1:2] + logs[2:3]


def write_packed(ref, h, state, log):
    size = ref.shape[1] - 16
    high = log.astype(BF16).astype(F32)
    middle = (log - high).astype(BF16).astype(F32)
    row = lax.broadcasted_iota(jnp.int32, (16, log.shape[1]), 0)
    logs = jnp.where(row == 0, high, jnp.where(row == 1, middle, log - high - middle))
    ref[h, :size, :] = state.astype(BF16)
    ref[h, size : size + 16, :] = logs.astype(BF16)


def row_kernel(x_ref, r0, r1, r2, r3, total_ref, inside_ref, inside_log_ref):
    x = x_ref[0]
    places = [lax.rem(x + 4 - k, 4) for k in range(4)]
    for h in range(r0.shape[0]):
        parts = [read_packed(r, h) for r in (r0, r1, r2, r3)]
        zero = jnp.zeros_like(parts[0][1])
        total, inside = jnp.zeros_like(parts[0][0]), jnp.zeros_like(parts[0][0])
        total_log, inside_log = zero, zero
        for k in range(4):
            early = places[k] < x
            after, within = zero, zero
            for m in range(4):
                later = places[m] > places[k]
                after = after + jnp.where(later, parts[m][1], 0.0)
                within = within + jnp.where(later & (places[m] < x), parts[m][1], 0.0)
            total = total + jnp.exp(after) * parts[k][0]
            total_log = total_log + parts[k][1]
            inside = inside + jnp.where(early, jnp.exp(within), 0.0) * parts[k][0]
            inside_log = inside_log + jnp.where(early, parts[k][1], 0.0)
        write_packed(total_ref, h, total, total_log)
        inside_ref[h] = inside
        inside_log_ref[h] = inside_log


def window_kernel(r0, r1, r2, r3, out_ref):
    for h in range(r0.shape[0]):
        state, log = read_packed(r3, h)
        for r in (r2, r1, r0):
            own, own_log = read_packed(r, h)
            state, log = own + jnp.exp(own_log) * state, log + own_log
        write_packed(out_ref, h, state, log)


def prior_kernel(r1, r5, inside_ref, inside_log_ref, carried_ref, out_ref):
    for h in range(r1.shape[0]):
        state = carried_ref[h]
        for r in (r5, r1):
            own, own_log = read_packed(r, h)
            state = own + jnp.exp(own_log) * state
        out_ref[h] = inside_ref[h] + jnp.exp(inside_log_ref[h]) * state


def on_device(
    tokens,
    norm_gain,
    router_weight,
    expert_ids,
    gate_weight,
    up_weight,
    down_weight,
    query_weight,
    key_weight,
    log_decay,
    carried_state,
    out_gain,
):
    span_rows = tokens.shape[0]
    width = tokens.shape[1]
    expert_count = router_weight.shape[1]
    top_count = expert_ids.shape[1]
    capacity = 7 * top_count * span_rows // (8 * expert_count)
    groups = lax.axis_size(EXPERT)
    mine = lax.axis_index(EXPERT)
    block_cols = width // groups
    rows_a, rows_b = ROWS_A, capacity - ROWS_A
    own_a, own_b, mix_weight, slots = route(
        mine.reshape(1), tokens, norm_gain[None], router_weight.T, expert_ids.T, rows_a, rows_b
    )

    hold = lax.optimization_barrier
    across = [shift(own_a, "x", k) for k in (1, -1, 2)]
    up1, down1 = shift(own_b, "z", 1), shift(own_b, "z", -1)
    up1, down1, *across = hold((up1, down1, *across))
    up2, down2 = shift(up1, "z", 1), shift(down1, "z", -1)
    all_a = lax.all_gather(stack([own_a, *across]), "z", axis=0, tiled=True)
    up2, down2 = hold((up2, down2))
    up3, down3 = shift(up2, "z", 1), shift(down2, "z", -1)
    up3, down3 = hold((up3, down3))
    up4 = shift(up3, "z", 1)
    all_b = stack([own_b, up1, down1, up2, down2, up3, down3, up4])
    half = all_b.shape[0] // 2
    all_b, late_tokens = hold((all_b, tokens))
    left_b, right_b = shift(all_b, "x", 1), shift(all_b, "x", -1)

    heads_local = log_decay.shape[0]
    key_size = query_weight.shape[1] // heads_local
    head_size = block_cols // heads_local
    tok_cols = lax.dynamic_slice_in_dim(late_tokens, mine * block_cols, block_cols, 1).astype(F32)
    keys_proj = (
        jnp.dot(late_tokens, key_weight, preferred_element_type=F32)
        .reshape(span_rows, heads_local, key_size)
        .transpose(1, 0, 2)
    )
    value_rows = tok_cols.reshape(span_rows, heads_local, head_size).transpose(1, 0, 2)
    running_state = jnp.cumsum(log_decay, axis=1)
    last_state = running_state[:, -1]
    scaled_keys = keys_proj * jnp.exp(last_state[:, None] - running_state)[:, :, None]
    block_state = jnp.einsum("wpl,wpg->wlg", scaled_keys, value_rows, precision=peak_error)
    packed = pack(block_state, last_state)

    row = [shift(packed, "x", k) for k in (1, 2, 3)]
    like = jax.ShapeDtypeStruct(packed.shape, BF16)
    state_shape = jax.ShapeDtypeStruct(carried_state.shape, F32)
    total, inside, inside_log = small_call(
        row_kernel,
        [like, state_shape, jax.ShapeDtypeStruct((heads_local, 1, head_size), F32)],
        lax.axis_index("x").reshape(1),
        packed,
        *row,
        scalars=1,
    )
    left_b, right_b, total = hold((left_b, right_b, total))
    before = [shift(total, "z", k, wrap=False) for k in (1, 2, 3)]
    run = small_call(window_kernel, like, total, *before)
    far_1, far_2 = shift(left_b[:half], "x", 1), shift(right_b[half:], "x", -1)

    weights = (gate_weight, up_weight, down_weight)
    halves = [half, half]
    part_b1, part_b2, part_l1, part_l2, part_r1, part_r2 = mlp(
        [all_b, left_b, right_b], halves * 3, *weights
    )
    all_a, far_1, far_2, part_b1, part_b2 = hold((all_a, far_1, far_2, part_b1, part_b2))
    part_a, part_f1, part_f2 = mlp([all_a, far_1, far_2], [all_a.shape[0]] + halves, *weights)

    sum_a = lax.psum_scatter(part_a, "z", scatter_dimension=0, tiled=True)
    relay_l, relay_r = shift(part_f1, "x", -1), shift(part_f2, "x", 1)
    rest_l, rest_r = shift(part_l2, "x", -1), shift(part_r1, "x", 1)
    relay_l, relay_r, rest_l, rest_r, run = hold((relay_l, relay_r, rest_l, rest_r, run))
    lead_l, lead_r = shift(add(part_l1, relay_l), "x", -1), shift(add(part_r2, relay_r), "x", 1)
    lead_l, lead_r = hold((lead_l, lead_r))
    sum_b = jnp.concatenate([add(part_b1, lead_l, rest_r), add(part_b2, rest_l, lead_r)])
    run_1, run_5 = hold((shift(run, "z", 1, wrap=False), shift(run, "z", 5, wrap=False)))
    spots = [rows_b * k for k in range(8)]
    back, fore = pick(sum_b, (spots[7], spots[6]), rows_b)
    back, fore = hold((shift(back, "z", -1), shift(fore, "z", 1)))
    back, fore = pick(sum_b, (spots[5], spots[4]), rows_b, (back, fore))
    back, fore = hold((shift(back, "z", -1), shift(fore, "z", 1)))
    back, fore = pick(sum_b, (spots[3], spots[2]), rows_b, (back, fore))
    back, fore, sum_a = hold((shift(back, "z", -1), shift(fore, "z", 1), sum_a))
    (back,) = pick(sum_b, (spots[1],), rows_b, (back,))
    back = shift(back, "z", -1)
    across = pick(sum_a, (rows_a, 2 * rows_a, 3 * rows_a), rows_a)
    across = [shift(v, "x", k) for v, k in zip(across, (-1, 1, 2))]
    pieces = finish([sum_a, *across], [sum_b, back, fore], groups, capacity)
    arrived = lax.all_to_all(pieces, EXPERT, split_axis=0, concat_axis=0, tiled=True)

    query_rows = (
        jnp.dot(tokens, query_weight, preferred_element_type=F32)
        .reshape(span_rows, heads_local, key_size)
        .transpose(1, 0, 2)
    )
    lower = jnp.arange(span_rows)[:, None] >= jnp.arange(span_rows)[None, :]
    gaps = running_state[:, :, None] - running_state[:, None, :]
    weights = jnp.where(lower[None], jnp.exp(jnp.minimum(gaps, 0.0)), 0.0)
    scores = jnp.einsum("htk,hsk->hts", query_rows, keys_proj, precision=peak_error) * weights
    output_rows = jnp.einsum("hts,hsv->htv", scores, value_rows, precision=peak_error)
    prior_state = small_call(
        prior_kernel, state_shape, run_1, run_5, inside, inside_log, carried_state
    )
    output_rows = output_rows + jnp.exp(running_state)[:, :, None] * jnp.einsum(
        "ezy,eyl->ezl", query_rows, prior_state, precision=peak_error
    )
    normed_out = output_rows * lax.rsqrt(
        jnp.mean(output_rows * output_rows, axis=2, keepdims=True) + head_epsilon
    )
    branch = normed_out.transpose(1, 0, 2).reshape(span_rows, block_cols) * out_gain
    teacher, student, loss = combine(
        arrived, mix_weight, slots, tok_cols.astype(BF16), branch
    )
    loss = lax.all_to_all(loss, EXPERT, split_axis=0, concat_axis=0, tiled=True)
    return teacher, student, jnp.sum(loss, axis=0) / width


def solution(mesh):
    finer = Mesh(mesh.devices.reshape(8, 4, 4, 2), ("z", "x", "y", "core"))
    in_specs = (
        P(SEQ, None),
        P(),
        P(),
        P(SEQ, None),
        P(EXPERT, None, SEQ),
        P(EXPERT, None, SEQ),
        P(EXPERT, SEQ, None),
        P(None, EXPERT),
        P(None, EXPERT),
        P(EXPERT, SEQ),
        P(EXPERT, None, None),
        P(EXPERT),
    )
    out_specs = (P(SEQ, EXPERT), P(SEQ, EXPERT), P(SEQ))
    return jax.shard_map(
        on_device, mesh=finer, in_specs=in_specs, out_specs=out_specs, check_vma=False
    )
```

```python
import functools

import jax
import jax.numpy as jnp
from jax import lax
from jax.experimental import pallas as pl
from jax.experimental.pallas import tpu as pltpu
from jax.sharding import Mesh
from jax.sharding import PartitionSpec as P

SEQ = ("z", "x")
EXPERT = ("y", "core")
ROWS_A = 14

norm_epsilon = 1e-05
head_epsilon = 1e-06
peak_error = lax.Precision.HIGHEST
F32 = jnp.float32
BF16 = jnp.bfloat16


def shift(value, axis, step, wrap=True):
    n = lax.axis_size(axis)
    pairs = [(i, (i + step) % n) for i in range(n) if wrap or 0 <= i + step < n]
    return lax.ppermute(value, axis, pairs)


def add(*terms):
    return sum(t.astype(F32) for t in terms).astype(BF16)


def mlp_kernel(n_in, n_out, tiles, *refs):
    x_refs, (gate_hbm, up_hbm, down_hbm) = refs[:n_in], refs[n_in : n_in + 3]
    out_refs = refs[n_in + 3 : n_in + 3 + n_out]
    scratch = refs[n_in + 3 + n_out :]
    x, gate, up, down, out, gates, ups, hidden, x_sem, w_sem, d_sem, o_sem = scratch
    tile = x.shape[1] // tiles

    def span_of(t):
        return pl.ds(pl.multiple_of(t * tile, tile), tile)

    def weight_copies(t):
        span = span_of(t)
        return (
            pltpu.make_async_copy(gate_hbm.at[0, span], gate.at[span], w_sem.at[0, t]),
            pltpu.make_async_copy(up_hbm.at[0, span], up.at[span], w_sem.at[1, t]),
        )

    def for_rows(t, act):
        span = span_of(t)
        at = 0
        for k, ref in enumerate(x_refs):
            size = ref.shape[0]
            act(
                pltpu.make_async_copy(
                    ref.at[:, span], x.at[pl.ds(at, size), span], x_sem.at[k, t]
                )
            )
            at += size

    down_copy = pltpu.make_async_copy(down_hbm.at[0], down, d_sem)

    @pl.loop(0, tiles)
    def _(t):
        for copy in weight_copies(t):
            copy.start()
        for_rows(t, lambda copy: copy.start())

    down_copy.start()
    gates[...] = jnp.zeros_like(gates)
    ups[...] = jnp.zeros_like(ups)

    @pl.loop(0, tiles)
    def _(t):
        for copy in weight_copies(t):
            copy.wait()
        for_rows(t, lambda copy: copy.wait())
        span = span_of(t)
        gates[...] += jnp.dot(x[:, span], gate[span], preferred_element_type=F32)
        ups[...] += jnp.dot(x[:, span], up[span], preferred_element_type=F32)

    v = gates[...]
    hidden[...] = (v / (1.0 + jnp.exp(-v)) * ups[...]).astype(BF16)
    down_copy.wait()

    def out_copies(t):
        span = span_of(t)
        at, copies = 0, []
        for k, ref in enumerate(out_refs):
            size = ref.shape[0]
            copies.append(
                pltpu.make_async_copy(
                    out.at[pl.ds(at, size), span], ref.at[:, span], o_sem.at[k, t]
                )
            )
            at += size
        return copies

    @pl.loop(0, tiles)
    def _(t):
        span = span_of(t)
        out[:, span] = jnp.dot(hidden[...], down[:, span], preferred_element_type=F32).astype(BF16)
        for copy in out_copies(t):
            copy.start()

    @pl.loop(0, tiles)
    def _(t):
        for copy in out_copies(t):
            copy.wait()


def mlp(arrays, sizes, gate, up, down):
    tiles, width, hidden = 4, gate.shape[1], gate.shape[2]
    total = sum(sizes)
    anywhere = pl.BlockSpec(memory_space=pltpu.MemorySpace.HBM)
    return pl.pallas_call(
        functools.partial(mlp_kernel, len(arrays), len(sizes), tiles),
        in_specs=[anywhere] * (len(arrays) + 3),
        out_specs=[anywhere] * len(sizes),
        out_shape=[jax.ShapeDtypeStruct((n, width), BF16) for n in sizes],
        scratch_shapes=[
            pltpu.VMEM((total, width), BF16),
            pltpu.VMEM((width, hidden), BF16),
            pltpu.VMEM((width, hidden), BF16),
            pltpu.VMEM((hidden, width), BF16),
            pltpu.VMEM((total, width), BF16),
            pltpu.VMEM((total, hidden), F32),
            pltpu.VMEM((total, hidden), F32),
            pltpu.VMEM((total, hidden), BF16),
            pltpu.SemaphoreType.DMA((len(arrays), tiles)),
            pltpu.SemaphoreType.DMA((2, tiles)),
            pltpu.SemaphoreType.DMA,
            pltpu.SemaphoreType.DMA((len(sizes), tiles)),
        ],
        compiler_params=pltpu.CompilerParams(vmem_limit_bytes=56 << 20),
        cost_estimate=pl.CostEstimate(
            flops=6 * total * width * hidden,
            bytes_accessed=4 * total * width + 6 * width * hidden,
            transcendentals=total * hidden,
        ),
    )(*arrays, gate, up, down)


def route_kernel(mine_ref, *refs):
    given, (a_ref, b_ref, mix_ref, slot_ref), held, sems = refs[:4], refs[4:8], refs[8:12], refs[12]
    copies = [pltpu.make_async_copy(g, h, sems.at[k]) for k, (g, h) in enumerate(zip(given, held))]
    for copy in copies:
        copy.start()
    for copy in copies:
        copy.wait()
    tok_ref, gain_ref, router_ref, ids_ref = held
    tok = tok_ref[...].astype(F32)
    scale = lax.rsqrt(jnp.mean(tok * tok, axis=1, keepdims=True) + norm_epsilon)
    normed = (tok * scale * gain_ref[...]).astype(BF16)
    contract = (((1,), (1,)), ((), ()))
    logits = lax.dot_general(router_ref[...], normed, contract, preferred_element_type=F32)
    experts, tokens = logits.shape
    expert = lax.broadcasted_iota(jnp.int32, logits.shape, 0)
    first, second = ids_ref[0:1, :] == expert, ids_ref[1:2, :] == expert
    chosen_first = jnp.sum(jnp.where(first, logits, 0.0), axis=0, keepdims=True)
    chosen_second = jnp.sum(jnp.where(second, logits, 0.0), axis=0, keepdims=True)
    share = 1.0 / (1.0 + jnp.exp(chosen_second - chosen_first))
    mix_ref[...] = jnp.where(first, share, 0.0) + jnp.where(second, 1.0 - share, 0.0)
    hits = first | second
    square = (tokens, tokens)
    earlier = lax.broadcasted_iota(jnp.int32, square, 0) < lax.broadcasted_iota(jnp.int32, square, 1)
    slots = jnp.dot(
        hits.astype(F32).astype(BF16), earlier.astype(F32).astype(BF16), preferred_element_type=F32
    ).astype(jnp.int32)
    slots = jnp.where(hits, slots, -1)
    slot_ref[...] = slots
    own = jnp.sum(jnp.where(expert == mine_ref[0], slots, 0), axis=0, keepdims=True)
    place = lax.broadcasted_iota(jnp.int32, (16, tokens), 0)
    for ref, start in ((a_ref, 0), (b_ref, a_ref.shape[0])):
        select = (own == place + start).astype(F32).astype(BF16)
        rows = jnp.dot(select, normed, preferred_element_type=F32).astype(BF16)
        ref[...] = rows[: ref.shape[0]]


def route(mine, tokens, gain, router, ids, rows_a, rows_b):
    count, width = tokens.shape
    experts = router.shape[0]
    vmem = pl.BlockSpec(memory_space=pltpu.VMEM)
    return pl.pallas_call(
        route_kernel,
        in_specs=[pl.BlockSpec(memory_space=pltpu.SMEM)]
        + [pl.BlockSpec(memory_space=pltpu.MemorySpace.HBM)] * 4,
        out_specs=[vmem] * 4,
        out_shape=[
            jax.ShapeDtypeStruct((rows_a, width), BF16),
            jax.ShapeDtypeStruct((rows_b, width), BF16),
            jax.ShapeDtypeStruct((experts, count), F32),
            jax.ShapeDtypeStruct((experts, count), jnp.int32),
        ],
        scratch_shapes=[pltpu.VMEM(v.shape, v.dtype) for v in (tokens, gain, router, ids)]
        + [pltpu.SemaphoreType.DMA((4,))],
        compiler_params=pltpu.CompilerParams(vmem_limit_bytes=58 << 20),
    )(mine, tokens, gain, router, ids)


def staged_kernel(kernel, scalars, count, *refs):
    given, rest = refs[scalars : scalars + count], refs[scalars + count :]
    held, sems = rest[-count - 1 : -1], rest[-1]
    copies = [pltpu.make_async_copy(g, h, sems.at[k]) for k, (g, h) in enumerate(zip(given, held))]
    for copy in copies:
        copy.start()
    for copy in copies:
        copy.wait()
    kernel(*refs[:scalars], *held, *rest[: -count - 1])


def small_call(kernel, out_shape, *args, scalars=0, scratch=()):
    arrays = args[scalars:]
    return pl.pallas_call(
        functools.partial(staged_kernel, kernel, scalars, len(arrays)),
        in_specs=[pl.BlockSpec(memory_space=pltpu.SMEM)] * scalars
        + [pl.BlockSpec(memory_space=pl.ANY)] * len(arrays),
        out_specs=jax.tree.map(lambda _: pl.BlockSpec(memory_space=pltpu.VMEM), out_shape),
        out_shape=out_shape,
        scratch_shapes=list(scratch)
        + [pltpu.VMEM(v.shape, v.dtype) for v in arrays]
        + [pltpu.SemaphoreType.DMA((len(arrays),))],
        compiler_params=pltpu.CompilerParams(vmem_limit_bytes=58 << 20),
    )(*args)


def stack_kernel(*refs):
    parts, out_ref, total = refs[:-2], refs[-2], refs[-1]
    rows = parts[0].shape[0]
    for k, part in enumerate(parts):
        total[k * rows : (k + 1) * rows, :] = part[...].astype(F32)
    out_ref[...] = total[...].astype(BF16)


def stack(parts):
    rows, width = parts[0].shape
    shape = (len(parts) * rows, width)
    return small_call(
        stack_kernel, jax.ShapeDtypeStruct(shape, BF16), *parts, scratch=[pltpu.VMEM(shape, F32)]
    )


def rows_from(ref, at, rows):
    low, high = at // 8 * 8, min(-(-(at + rows) // 8) * 8, ref.shape[0])
    return ref[low:high, :].astype(F32)[at - low : at - low + rows]


def pick_kernel(ats, summed, value_ref, *refs):
    terms, outs = refs[:summed], refs[summed:]
    for k, (at, out) in enumerate(zip(ats, outs)):
        rows = rows_from(value_ref, at, out.shape[0])
        if summed:
            rows = rows + terms[k][...].astype(F32)
        out[...] = rows.astype(BF16)


def pick(value, ats, rows, terms=()):
    vmem = pl.BlockSpec(memory_space=pltpu.VMEM)
    return pl.pallas_call(
        functools.partial(pick_kernel, ats, len(terms)),
        in_specs=[vmem] * (1 + len(terms)),
        out_specs=[vmem] * len(ats),
        out_shape=[jax.ShapeDtypeStruct((rows, value.shape[1]), BF16)] * len(ats),
        compiler_params=pltpu.CompilerParams(vmem_limit_bytes=16 << 20),
    )(value, *terms)


def finish_kernel(n_a, *refs):
    parts_a, parts_b, out_ref, total = refs[:n_a], refs[n_a:-2], refs[-2], refs[-1]
    groups, rows, cols = out_ref.shape
    rows_a = parts_a[1].shape[0]
    total[:rows_a, :] = sum(rows_from(p, 0, rows_a) for p in parts_a)
    total[rows_a:rows, :] = sum(rows_from(p, 0, rows - rows_a) for p in parts_b)
    for g in range(groups):
        out_ref[g, :, :] = total[:rows, g * cols : (g + 1) * cols].astype(BF16)


def finish(parts_a, parts_b, groups, rows):
    width = parts_a[0].shape[1]
    vmem = pl.BlockSpec(memory_space=pltpu.VMEM)
    return pl.pallas_call(
        functools.partial(finish_kernel, len(parts_a)),
        in_specs=[vmem] * (len(parts_a) + len(parts_b)),
        out_specs=vmem,
        out_shape=jax.ShapeDtypeStruct((groups, rows, width // groups), BF16),
        scratch_shapes=[pltpu.VMEM((32, width), F32)],
        compiler_params=pltpu.CompilerParams(vmem_limit_bytes=16 << 20),
    )(*parts_a, *parts_b)


def combine_kernel(arrived_ref, mix_ref, slot_ref, tok_ref, branch_ref, teach_ref, stud_ref, loss_ref):
    experts, rows, cols = arrived_ref.shape
    tokens = tok_ref.shape[0]
    place = lax.broadcasted_iota(jnp.int32, (rows, tokens), 0)
    contract = (((0,), (0,)), ((), ()))
    mixed = jnp.zeros((tokens, cols), F32)
    for e in range(experts):
        weigh = jnp.where(slot_ref[e : e + 1, :] == place, mix_ref[e : e + 1, :], 0.0)
        mixed = mixed + lax.dot_general(
            weigh,
            arrived_ref[e].astype(F32),
            contract,
            precision=peak_error,
            preferred_element_type=F32,
        )
    tok = tok_ref[...].astype(F32)
    teacher, student = tok + mixed, tok + branch_ref[...]
    teach_ref[...] = teacher.astype(BF16)
    stud_ref[...] = student.astype(BF16)
    gap = student - teacher
    loss_ref[...] = lax.dot_general(
        jnp.ones((experts, cols), F32),
        gap * gap,
        (((1,), (1,)), ((), ())),
        precision=peak_error,
        preferred_element_type=F32,
    )


def combine(arrived, mix, slots, tok_cols, branch):
    experts, _, cols = arrived.shape
    count = tok_cols.shape[0]
    vmem = pl.BlockSpec(memory_space=pltpu.VMEM)
    return pl.pallas_call(
        combine_kernel,
        in_specs=[vmem] * 5,
        out_specs=[vmem] * 3,
        out_shape=[
            jax.ShapeDtypeStruct((count, cols), BF16),
            jax.ShapeDtypeStruct((count, cols), BF16),
            jax.ShapeDtypeStruct((experts, count), F32),
        ],
        compiler_params=pltpu.CompilerParams(vmem_limit_bytes=16 << 20),
    )(arrived, mix, slots, tok_cols, branch)


def split_log(value):
    high = lax.reduce_precision(value, 8, 7)
    middle = lax.reduce_precision(value - high, 8, 7)
    return jnp.stack([high, middle, value - high - middle], axis=1)


def pack(state, log):
    heads, keys, size = state.shape
    logs = jnp.broadcast_to(split_log(log)[:, :, None], (heads, 3, size))
    logs = jnp.pad(logs, ((0, 0), (0, 13), (0, 0)))
    return jnp.concatenate([state, logs], axis=1).astype(BF16)


def read_packed(ref, h):
    size = ref.shape[1] - 16
    logs = ref[h, size : size + 16, :].astype(F32)
    return ref[h, :size, :].astype(F32), logs[0:1] + logs[1:2] + logs[2:3]


def write_packed(ref, h, state, log):
    size = ref.shape[1] - 16
    high = log.astype(BF16).astype(F32)
    middle = (log - high).astype(BF16).astype(F32)
    row = lax.broadcasted_iota(jnp.int32, (16, log.shape[1]), 0)
    logs = jnp.where(row == 0, high, jnp.where(row == 1, middle, log - high - middle))
    ref[h, :size, :] = state.astype(BF16)
    ref[h, size : size + 16, :] = logs.astype(BF16)


def row_kernel(x_ref, r0, r1, r2, r3, total_ref, inside_ref, inside_log_ref):
    x = x_ref[0]
    places = [lax.rem(x + 4 - k, 4) for k in range(4)]
    for h in range(r0.shape[0]):
        parts = [read_packed(r, h) for r in (r0, r1, r2, r3)]
        zero = jnp.zeros_like(parts[0][1])
        total, inside = jnp.zeros_like(parts[0][0]), jnp.zeros_like(parts[0][0])
        total_log, inside_log = zero, zero
        for k in range(4):
            early = places[k] < x
            after, within = zero, zero
            for m in range(4):
                later = places[m] > places[k]
                after = after + jnp.where(later, parts[m][1], 0.0)
                within = within + jnp.where(later & (places[m] < x), parts[m][1], 0.0)
            total = total + jnp.exp(after) * parts[k][0]
            total_log = total_log + parts[k][1]
            inside = inside + jnp.where(early, jnp.exp(within), 0.0) * parts[k][0]
            inside_log = inside_log + jnp.where(early, parts[k][1], 0.0)
        write_packed(total_ref, h, total, total_log)
        inside_ref[h] = inside
        inside_log_ref[h] = inside_log


def window_kernel(r0, r1, r2, r3, out_ref):
    for h in range(r0.shape[0]):
        state, log = read_packed(r3, h)
        for r in (r2, r1, r0):
            own, own_log = read_packed(r, h)
            state, log = own + jnp.exp(own_log) * state, log + own_log
        write_packed(out_ref, h, state, log)


def prior_kernel(r1, r5, inside_ref, inside_log_ref, carried_ref, out_ref):
    for h in range(r1.shape[0]):
        state = carried_ref[h]
        for r in (r5, r1):
            own, own_log = read_packed(r, h)
            state = own + jnp.exp(own_log) * state
        out_ref[h] = inside_ref[h] + jnp.exp(inside_log_ref[h]) * state


def on_device(
    tokens,
    norm_gain,
    router_weight,
    expert_ids,
    gate_weight,
    up_weight,
    down_weight,
    query_weight,
    key_weight,
    log_decay,
    carried_state,
    out_gain,
):
    span_rows = tokens.shape[0]
    width = tokens.shape[1]
    expert_count = router_weight.shape[1]
    top_count = expert_ids.shape[1]
    capacity = 7 * top_count * span_rows // (8 * expert_count)
    groups = lax.axis_size(EXPERT)
    mine = lax.axis_index(EXPERT)
    block_cols = width // groups
    rows_a, rows_b = ROWS_A, capacity - ROWS_A
    own_a, own_b, mix_weight, slots = route(
        mine.reshape(1), tokens, norm_gain[None], router_weight.T, expert_ids.T, rows_a, rows_b
    )

    heads_local = log_decay.shape[0]
    key_size = query_weight.shape[1] // heads_local
    head_size = block_cols // heads_local
    tok_cols = lax.dynamic_slice_in_dim(tokens, mine * block_cols, block_cols, 1).astype(F32)
    keys_proj = (
        jnp.dot(tokens, key_weight, preferred_element_type=F32)
        .reshape(span_rows, heads_local, key_size)
        .transpose(1, 0, 2)
    )
    value_rows = tok_cols.reshape(span_rows, heads_local, head_size).transpose(1, 0, 2)
    running_state = jnp.cumsum(log_decay, axis=1)
    last_state = running_state[:, -1]
    scaled_keys = keys_proj * jnp.exp(last_state[:, None] - running_state)[:, :, None]
    block_state = jnp.einsum("wpl,wpg->wlg", scaled_keys, value_rows, precision=peak_error)
    packed = pack(block_state, last_state)

    hold = lax.optimization_barrier
    across = [shift(own_a, "x", k) for k in (1, -1, 2)]
    up1, down1 = shift(own_b, "z", 1), shift(own_b, "z", -1)
    up1, down1, *across = hold((up1, down1, *across))
    up2, down2 = shift(up1, "z", 1), shift(down1, "z", -1)
    all_a = lax.all_gather(stack([own_a, *across]), "z", axis=0, tiled=True)
    up2, down2, packed = hold((up2, down2, packed))
    up3, down3 = shift(up2, "z", 1), shift(down2, "z", -1)
    row = [shift(packed, "x", k) for k in (1, 2, 3)]
    up3, down3 = hold((up3, down3))
    up4 = shift(up3, "z", 1)
    up4, *row = hold((up4, *row))
    like = jax.ShapeDtypeStruct(packed.shape, BF16)
    state_shape = jax.ShapeDtypeStruct(carried_state.shape, F32)
    total, inside, inside_log = small_call(
        row_kernel,
        [like, state_shape, jax.ShapeDtypeStruct((heads_local, 1, head_size), F32)],
        lax.axis_index("x").reshape(1),
        packed,
        *row,
        scalars=1,
    )
    all_b = stack([own_b, up1, down1, up2, down2, up3, down3, up4])
    all_b, total = hold((all_b, total))
    half = all_b.shape[0] // 2
    left_b, right_b = shift(all_b, "x", 1), shift(all_b, "x", -1)
    before = [shift(total, "z", k, wrap=False) for k in (1, 2, 3)]
    run = small_call(window_kernel, like, total, *before)
    left_b, right_b, run = hold((left_b, right_b, run))
    far_1, far_2 = shift(left_b[:half], "x", 1), shift(right_b[half:], "x", -1)
    run_1, run_5 = shift(run, "z", 1, wrap=False), shift(run, "z", 5, wrap=False)

    weights = (gate_weight, up_weight, down_weight)
    halves = [half, half]
    part_b1, part_b2, part_l1, part_l2, part_r1, part_r2 = mlp(
        [all_b, left_b, right_b], halves * 3, *weights
    )
    all_a, far_1, far_2, run_1, run_5 = hold((all_a, far_1, far_2, run_1, run_5))
    part_a, part_f1, part_f2 = mlp([all_a, far_1, far_2], [all_a.shape[0]] + halves, *weights)

    sum_a = lax.psum_scatter(part_a, "z", scatter_dimension=0, tiled=True)
    relay_l, relay_r = shift(part_f1, "x", -1), shift(part_f2, "x", 1)
    rest_l, rest_r = shift(part_l2, "x", -1), shift(part_r1, "x", 1)
    relay_l, relay_r = hold((relay_l, relay_r))
    lead_l, lead_r = shift(add(part_l1, relay_l), "x", -1), shift(add(part_r2, relay_r), "x", 1)
    lead_l, lead_r, rest_l, rest_r = hold((lead_l, lead_r, rest_l, rest_r))
    sum_b = jnp.concatenate([add(part_b1, lead_l, rest_r), add(part_b2, rest_l, lead_r)])
    spots = [rows_b * k for k in range(8)]
    back, fore = pick(sum_b, (spots[7], spots[6]), rows_b)
    back, fore = hold((shift(back, "z", -1), shift(fore, "z", 1)))
    back, fore = pick(sum_b, (spots[5], spots[4]), rows_b, (back, fore))
    back, fore = hold((shift(back, "z", -1), shift(fore, "z", 1)))
    back, fore = pick(sum_b, (spots[3], spots[2]), rows_b, (back, fore))
    back, fore, sum_a = hold((shift(back, "z", -1), shift(fore, "z", 1), sum_a))
    (back,) = pick(sum_b, (spots[1],), rows_b, (back,))
    back = shift(back, "z", -1)
    across = pick(sum_a, (rows_a, 2 * rows_a, 3 * rows_a), rows_a)
    across = [shift(v, "x", k) for v, k in zip(across, (-1, 1, 2))]
    pieces = finish([sum_a, *across], [sum_b, back, fore], groups, capacity)
    arrived = lax.all_to_all(pieces, EXPERT, split_axis=0, concat_axis=0, tiled=True)

    query_rows = (
        jnp.dot(tokens, query_weight, preferred_element_type=F32)
        .reshape(span_rows, heads_local, key_size)
        .transpose(1, 0, 2)
    )
    lower = jnp.arange(span_rows)[:, None] >= jnp.arange(span_rows)[None, :]
    gaps = running_state[:, :, None] - running_state[:, None, :]
    weights = jnp.where(lower[None], jnp.exp(jnp.minimum(gaps, 0.0)), 0.0)
    scores = jnp.einsum("htk,hsk->hts", query_rows, keys_proj, precision=peak_error) * weights
    output_rows = jnp.einsum("hts,hsv->htv", scores, value_rows, precision=peak_error)
    prior_state = small_call(
        prior_kernel, state_shape, run_1, run_5, inside, inside_log, carried_state
    )
    output_rows = output_rows + jnp.exp(running_state)[:, :, None] * jnp.einsum(
        "ezy,eyl->ezl", query_rows, prior_state, precision=peak_error
    )
    normed_out = output_rows * lax.rsqrt(
        jnp.mean(output_rows * output_rows, axis=2, keepdims=True) + head_epsilon
    )
    branch = normed_out.transpose(1, 0, 2).reshape(span_rows, block_cols) * out_gain
    teacher, student, loss = combine(
        arrived, mix_weight, slots, tok_cols.astype(BF16), branch
    )
    loss = lax.all_to_all(loss, EXPERT, split_axis=0, concat_axis=0, tiled=True)
    return teacher, student, jnp.sum(loss, axis=0) / width


def solution(mesh):
    finer = Mesh(mesh.devices.reshape(8, 4, 4, 2), ("z", "x", "y", "core"))
    in_specs = (
        P(SEQ, None),
        P(),
        P(),
        P(SEQ, None),
        P(EXPERT, None, SEQ),
        P(EXPERT, None, SEQ),
        P(EXPERT, SEQ, None),
        P(None, EXPERT),
        P(None, EXPERT),
        P(EXPERT, SEQ),
        P(EXPERT, None, None),
        P(EXPERT),
    )
    out_specs = (P(SEQ, EXPERT), P(SEQ, EXPERT), P(SEQ))
    return jax.shard_map(
        on_device, mesh=finer, in_specs=in_specs, out_specs=out_specs, check_vma=False
    )
```
